32 devices in a mesh: row: 16 (over z, y, core), col: 2 (over x).
Axes of the slice: x: 2, y: 2, z: 4, core: 2. Of those that a mesh axis runs over, the one named last changes fastest.
Arguments:
- charges: bfloat16 [64, 131072], P(None, ('row', 'col')), may hold values from -6 to 6
- points: float32 [3, 131072], P(None, ('row', 'col')), may hold values from 0 to 64, as said below
- leaf_basis: bfloat16 [32, 131072], P(None, ('row', 'col')), may hold values from -0.75 to 0.75
- transfer_one: bfloat16 [2048, 32, 32], P(('row', 'col')), may hold values from -0.5 to 0.5
- transfer_two: bfloat16 [256, 32, 32], P(('row', 'col')), may hold values from -0.5 to 0.5
- couple_one: bfloat16 [256, 12, 32, 32], P(('row', 'col')), may hold values from -0.3125 to 0.3125
- couple_two: bfloat16 [32, 16, 32, 32], P(('row', 'col')), may hold values from -0.25 to 0.25
- near_list: int32 [2048, 27], P(('row', 'col')), may hold values from -1 to 2047, as said below
- list_one: int32 [256, 12], P(('row', 'col')), may hold values from -1 to 255, as said below
- list_two: int32 [32, 16], P(('row', 'col')), may hold values from 0 to 31
Outputs:
- potential: bfloat16 [64, 131072], P(None, ('row', 'col'))
The draws below stay inside these ranges and needn't reach their ends.
Inputs may be any that keep to these rules, and one draw needn't show every extreme that they name: `points`: point p of the leaf at grid position (x, y, z) lies in the unit cube [x, x + 1) x [y, y + 1) x [z, z + 1). `near_list`: slot s = 9 (dz + 1) + 3 (dy + 1) + (dx + 1), with dx, dy, dz in -1, 0, 1, names the leaf at grid offset (dx, dy, dz) from the row's leaf, or is -1; it is -1 wherever that position lies outside the grid; slot 13 names the leaf itself. `list_one`: in each row the named nodes come first and the -1 entries last, at least 6 named; each named node has the same index // 16 as the row's node.
All inputs are finite; a program needn't handle non-finite values.
Results may differ from the reference program's by a relative error of at most 0.0053.
Values may be sent and summed in bfloat16 or wider, within the bound.
No kernel may reach another device: no remote copies, remote signals or barrier semaphores. Data moves between devices by JAX's collectives and lax.ppermute only.
A program may use at most 128 MiB of HBM per device.

```python
import jax
import jax.numpy as jnp
from jax import lax

PTS = 64
RANK = 32
RHS = 64
BX = 4
BY = 4
NEAR = 27
COUP1 = 12
TOPC = 16
LEAF_DEV = 64
GX = 8
GY = 64
GZ = 4
LEAVES = 2048
POINTS = 131072
NODES1 = 256
NODES2 = 32
BLOCK1 = 16


def leaf_place(index):
    column_count = GX // BX
    device = index // LEAF_DEV
    local = index % LEAF_DEV
    row_block = device // column_count
    col_block = device % column_count
    upper = local // 64
    lower = local % 64
    xpos = col_block * BX + lower // 8 % 2 * 2 + lower % 2
    ypos = row_block * BY + lower // 16 % 2 * 2 + lower // 2 % 2
    zpos = upper * 4 + lower // 32 % 2 * 2 + lower // 4 % 2
    return (xpos, ypos, zpos)


def leaf_number(xpos, ypos, zpos):
    column_count = GX // BX
    col_block = xpos // BX
    row_block = ypos // BY
    local_x = xpos % BX
    local_y = ypos % BY
    upper = zpos // 4
    local_z = zpos % 4
    lower = local_x % 2 + 2 * (local_y % 2) + 4 * (local_z % 2) + 8 * (local_x // 2) + 16 * (local_y // 2) + 32 * (local_z // 2)
    return (row_block * column_count + col_block) * LEAF_DEV + upper * 64 + lower


def draw_points(key, part):
    inner_key = jax.random.fold_in(key, 31)
    pick_key = jax.random.fold_in(key, 32)
    close_key = jax.random.fold_in(key, 33)
    leaf_index = jnp.arange(POINTS, dtype=jnp.int32) // PTS
    xpos, ypos, zpos = leaf_place(leaf_index)
    corner = jnp.stack([xpos, ypos, zpos]).astype(jnp.float32)
    spread_inside = jax.random.uniform(inner_key, (3, POINTS), jnp.float32, 0.0, 0.999)
    close_offset = 0.03 * jax.random.uniform(close_key, (3, POINTS), jnp.float32, 0.0, 1.0)
    picked = jax.random.randint(pick_key, (3, POINTS), 0, 4, dtype=jnp.int32)
    inside = jnp.where(picked == 0, close_offset, jnp.where(picked == 1, 0.999 - close_offset, spread_inside))
    return corner + inside


def draw_near_list(key, part):
    drop_key = jax.random.fold_in(key, 41)
    leaf_index = jnp.arange(LEAVES, dtype=jnp.int32)[:, None]
    slot = jnp.arange(27, dtype=jnp.int32)[None, :]
    step_x = slot % 3 - 1
    step_y = slot // 3 % 3 - 1
    step_z = slot // 9 - 1
    xpos, ypos, zpos = leaf_place(leaf_index)
    near_x = xpos + step_x
    near_y = ypos + step_y
    near_z = zpos + step_z
    inside = (near_x >= 0) & (near_x < GX) & (near_y >= 0) & (near_y < GY) & (near_z >= 0) & (near_z < GZ)
    keep = jax.random.randint(drop_key, (LEAVES, 27), 0, 4, dtype=jnp.int32) > 0
    keep = keep | (slot == 13)
    target = leaf_number(jnp.clip(near_x, 0, GX - 1), jnp.clip(near_y, 0, GY - 1), jnp.clip(near_z, 0, GZ - 1))
    return jnp.where(inside & keep, target, -1).astype(jnp.int32)


def draw_list_one(key, part):
    first_key = jax.random.fold_in(key, 21)
    second_key = jax.random.fold_in(key, 22)
    node_index = jnp.arange(NODES1, dtype=jnp.int32)[:, None]
    group_start = node_index // BLOCK1 * BLOCK1
    partner = group_start + jax.random.randint(first_key, (NODES1, COUP1), 0, BLOCK1, dtype=jnp.int32)
    filled = jax.random.randint(second_key, (NODES1, 1), COUP1 // 2, COUP1 + 1, dtype=jnp.int32)
    slot_index = jnp.arange(COUP1, dtype=jnp.int32)[None, :]
    return jnp.where(slot_index < filled, partner, -1).astype(jnp.int32)


def set_ends(result, key, low, largest):
    longest = result.shape.index(max(result.shape))
    spots = []
    for shift in (0, 1):
        where = [jax.random.randint(jax.random.fold_in(key, axis), (), 0, length) for axis, length in enumerate(result.shape)]
        where[longest] = (where[longest] + shift) % result.shape[longest]
        spots.append(tuple(where))
    return result.at[spots[0]].set(low).at[spots[1]].set(largest)


def block_levels(rng, extent, split, low, top_value):
    level, own = 1.0, jax.random.fold_in(rng, 6)
    for axis_at, shards_of in split:
        steps = jnp.exp(jax.random.uniform(jax.random.fold_in(own, axis_at), (shards_of,), jnp.float32, low / len(split), top_value / len(split)))
        level = level * jnp.repeat(steps, extent[axis_at] // shards_of).reshape([-1 if axis == axis_at else 1 for axis in range(len(extent))])
    return level


def gaussian(key, dims, width, most, split=(), kind=jnp.bfloat16):
    result = jax.random.normal(key, dims, jnp.float32) * width
    if len(split) > 0:
        result = block_levels(key, dims, split, -0.22, 0.18) * result
    return jnp.clip(result, min=-most, max=most).astype(kind)


def setup_inputs(seed: int = 0) -> dict:
    streams_of = jax.random.split(jax.random.key(seed), 11)
    charges = gaussian(streams_of[0], (RHS, POINTS), 1.0, 6.0, ((1, 32),))
    points = draw_points(jax.random.fold_in(streams_of[10], 71), 0)
    leaf_basis = gaussian(streams_of[2], (RANK, POINTS), PTS ** -0.5, 0.75, ((1, 32),))
    transfer_one = gaussian(streams_of[3], (LEAVES, RANK, RANK), (4 * RANK) ** -0.5, 0.5, ((0, 32),))
    transfer_two = gaussian(streams_of[4], (NODES1, RANK, RANK), (4 * RANK) ** -0.5, 0.5, ((0, 32),))
    couple_one = gaussian(streams_of[5], (NODES1, COUP1, RANK, RANK), (COUP1 * RANK) ** -0.5, 0.3125, ((0, 32),))
    couple_two = gaussian(streams_of[6], (NODES2, TOPC, RANK, RANK), (TOPC * RANK) ** -0.5, 0.25, ((0, 32),))
    near_list = draw_near_list(jax.random.fold_in(streams_of[10], 71), 0)
    list_one = draw_list_one(jax.random.fold_in(streams_of[10], 71), 0)
    list_two = set_ends(jax.random.randint(streams_of[9], (NODES2, TOPC), 0, NODES2), jax.random.fold_in(streams_of[9], 1), 0, NODES2 - 1).astype(jnp.int32)
    return {"charges": charges, "points": points, "leaf_basis": leaf_basis, "transfer_one": transfer_one, "transfer_two": transfer_two, "couple_one": couple_one, "couple_two": couple_two, "near_list": near_list, "list_one": list_one, "list_two": list_two}


softening = 0.0025

def leaf_block(source, remote, values, active):
    distance = source[:, None, :, :, None] - remote[:, :, :, None, :]
    kernel = (active[:, :, None, None] / jnp.sqrt(lax.optimization_barrier(jnp.sum(distance * distance, axis=2)) + softening)).astype(jnp.bfloat16)
    return jnp.einsum('lsij,lsrj->lri', kernel.astype(jnp.float32), values.astype(jnp.float32))

def reference(charges, points, leaf_basis, transfer_one, transfer_two, couple_one, couple_two, near_list, list_one, list_two):
    charge_leaf = charges.reshape(RHS, LEAVES, PTS).transpose(1, 0, 2)
    point_leaf = points.reshape(3, LEAVES, PTS).transpose(1, 0, 2)
    basis_leaf = leaf_basis.reshape(RANK, LEAVES, PTS).astype(jnp.float32)

    def near_step(block_index):
        offset = block_index * 64
        leaf_ids = lax.dynamic_slice_in_dim(near_list, offset, 64, 0)
        active = (leaf_ids >= 0).astype(jnp.float32)
        safe_ids = jnp.maximum(leaf_ids, 0)
        source = lax.dynamic_slice_in_dim(point_leaf, offset, 64, 0)
        return leaf_block(source, point_leaf[safe_ids], charge_leaf[safe_ids], active)
    near_part = lax.map(near_step, jnp.arange(LEAVES // 64, dtype=jnp.int32)).reshape(LEAVES, RHS, PTS)
    coef_leaf = jnp.einsum('kln,lrn->lkr', basis_leaf, charge_leaf.astype(jnp.float32)).astype(jnp.bfloat16)
    lifted = jnp.einsum('lab,lar->lbr', transfer_one.astype(jnp.float32), coef_leaf.astype(jnp.float32))
    coef_one = lifted.reshape(NODES1, 8, RANK, RHS).sum(axis=1).astype(jnp.bfloat16)
    lifted_two = jnp.einsum('lab,lar->lbr', transfer_two.astype(jnp.float32), coef_one.astype(jnp.float32))
    coef_two = lifted_two.reshape(NODES2, 8, RANK, RHS).sum(axis=1).astype(jnp.bfloat16)

    def couple_step(block_index):
        offset = block_index * 64
        partner_ids = lax.dynamic_slice_in_dim(list_one, offset, 64, 0)
        matrices = lax.dynamic_slice_in_dim(couple_one, offset, 64, 0)
        active = (partner_ids >= 0).astype(jnp.bfloat16)
        partner = coef_one[jnp.maximum(partner_ids, 0)] * active[:, :, None, None]
        return jnp.einsum('psab,psbr->par', matrices.astype(jnp.float32), partner.astype(jnp.float32))
    field_one = lax.map(couple_step, jnp.arange(NODES1 // 64, dtype=jnp.int32)).reshape(NODES1, RANK, RHS)
    field_two = jnp.einsum('psab,psbr->par', couple_two.astype(jnp.float32), coef_two[list_two].astype(jnp.float32))
    down_one = field_one + jnp.einsum('pab,pbr->par', transfer_two.astype(jnp.float32), jnp.repeat(field_two, 8, axis=0), precision=lax.Precision.HIGHEST)
    down_leaf = jnp.einsum('lab,lbr->lar', transfer_one.astype(jnp.float32), jnp.repeat(down_one, 8, axis=0), precision=lax.Precision.HIGHEST).astype(jnp.bfloat16)
    far_part = jnp.einsum('kln,lkr->lrn', basis_leaf, down_leaf.astype(jnp.float32))
    potential = near_part * (NEAR * PTS) ** (-0.5) + far_part
    return potential.transpose(1, 0, 2).reshape(RHS, LEAVES * PTS).astype(jnp.bfloat16)
```

```python
import functools

import jax
import jax.numpy as jnp
import numpy as np
from jax import lax
from jax.experimental import pallas as pl
from jax.experimental.pallas import tpu as pltpu
from jax.sharding import PartitionSpec as P

NEAR = 27
SIDE = 4
SOFTENING = 0.0025
F32 = jnp.float32
BF16 = jnp.bfloat16
NT = (((1,), (1,)), ((), ()))
TN = (((0,), (0,)), ((), ()))
NN = (((1,), (0,)), ((), ()))


def dot(a, b, dims=NN):
    return lax.dot_general(a, b, dims, preferred_element_type=F32)


def split2(v):
    hi = v.astype(BF16)
    lo = (v - hi.astype(F32)).astype(BF16)
    return hi, lo


def tile_of(z, y, x1):
    return (z // 4) * 32 + (z // 2 % 2) * 16 + (y // 2) * 8 + x1 * 4 + (z % 2) * 2 + (y % 2)


def lower_half(shape):
    return lax.broadcasted_iota(jnp.int32, shape, len(shape) - 1) % 128 < 64


def swap_matrix():
    a = lax.broadcasted_iota(jnp.int32, (128, 128), 0)
    b = lax.broadcasted_iota(jnp.int32, (128, 128), 1)
    return jnp.where((a + 64) % 128 == b, 1.0, 0.0).astype(BF16)


def block_basis(basis):
    rank, width = basis.shape
    leaf = lax.broadcasted_iota(jnp.int32, (rank, width), 1) // 64
    zero = jnp.zeros_like(basis)
    return jnp.concatenate([jnp.where(leaf == k, basis, zero) for k in range(8)], axis=0)


def up_kernel(merge, depth, q_ref, pts_ref, basis_ref, t1_ref, t2_ref, pb_ref, xpay_ref, coef_ref, *more):
    row, col = lax.axis_index("row"), lax.axis_index("col")
    columns = q_ref.shape[1]
    nodes = columns // 512
    centre = (
        (SIDE * col + SIDE // 2).astype(F32),
        (SIDE * row + SIDE // 2).astype(F32),
        jnp.float32(depth / 2),
    )
    index = lax.broadcasted_iota(jnp.int32, (16, columns), 0)
    rows = jnp.zeros((16, columns), F32)
    for c in range(3):
        local = pts_ref[c : c + 1, :] - centre[c]
        hi, lo = split2(local)
        rows = jnp.where(index == c, hi.astype(F32), rows)
        rows = jnp.where(index == c + 3, lo.astype(F32), rows)
    pb_ref[...] = rows.astype(BF16)
    swap = swap_matrix()
    low = lower_half((80, 128))
    for z in range(depth):
        for y1 in range(2):
            out = z * 2 + y1

            def tile(y, x1):
                at = tile_of(z, y, x1) * 128
                return jnp.concatenate([q_ref[:, at : at + 128], pb_ref[:, at : at + 128]], axis=0)

            high = jnp.where(low, dot(tile(2 * y1, 1), swap).astype(BF16), tile(2 * y1 + 1, 1))
            base = jnp.where(low, tile(2 * y1, 0), dot(tile(2 * y1 + 1, 0), swap).astype(BF16))
            if merge:
                xpay_ref[:, out * 128 : out * 128 + 128] = jnp.where(col == 0, high, base)
            else:
                xpay_ref[:, out * 128 : out * 128 + 128] = high
                more[0][:, out * 128 : out * 128 + 128] = base
    ones = []
    for n in range(nodes):
        chunk = slice(512 * n, 512 * n + 512)
        leaf = dot(block_basis(basis_ref[:, chunk]), q_ref[:, chunk], NT).astype(BF16)
        ones.append(dot(t1_ref[256 * n : 256 * n + 256, :], leaf, TN).astype(BF16))
        coef_ref[32 * n : 32 * n + 32, :] = ones[-1]
    for m in range(nodes // 8):
        part = jnp.concatenate(ones[8 * m : 8 * m + 8], axis=0)
        two = dot(t2_ref[256 * m : 256 * m + 256, :], part, TN).astype(BF16)
        coef_ref[32 * (nodes + m) : 32 * (nodes + m) + 32, :] = two


def pack_kernel(merge, depth, q_ref, pb_ref, *refs):
    if merge:
        xr_ref, h_ref, even_ref, odd_ref = refs
    else:
        xl_ref, xr_ref, h_ref, even_ref, odd_ref = refs
    row, col = lax.axis_index("row"), lax.axis_index("col")
    swap = swap_matrix()
    low = lower_half((80, 128))
    for z in range(depth):
        for y1 in range(2):
            at = (z * 2 + y1) * 128
            right = xr_ref[:, at : at + 128]
            left = right if merge else xl_ref[:, at : at + 128]
            h0 = jnp.where(low, right, dot(left, swap).astype(BF16))
            h1 = jnp.where(low, dot(right, swap).astype(BF16), left)
            at = (z * 4 + 2 * y1) * 128
            h_ref[:, at : at + 128] = h0
            h_ref[:, at + 128 : at + 256] = h1
    even = row % 2 == 0
    for z in range(depth):
        for k in range(3):

            def piece(y):
                if k < 2:
                    at = tile_of(z, y, k) * 128
                    return jnp.concatenate([q_ref[:, at : at + 128], pb_ref[:, at : at + 128]], axis=0)
                at = (z * 4 + y) * 128
                return h_ref[:, at : at + 128]

            first, last = piece(0), piece(SIDE - 1)
            at = (z * 3 + k) * 128
            even_ref[:, at : at + 128] = jnp.where(even, last, first)
            odd_ref[:, at : at + 128] = jnp.where(even, first, last)


def features(hi_lo, shift, scale):
    x = [hi_lo[c : c + 1, :] + hi_lo[c + 3 : c + 4, :] + shift[c] for c in range(3)]
    norm = x[0] * x[0] + x[1] * x[1] + x[2] * x[2]
    pairs = [split2(v) for v in x]
    hi = [a.astype(F32) * scale for a, _ in pairs]
    lo = [b.astype(F32) * scale for _, b in pairs]
    return norm, hi, lo


def split3(v):
    a = v.astype(BF16).astype(F32)
    b = (v - a).astype(BF16).astype(F32)
    c = (v - a - b).astype(BF16).astype(F32)
    return a, b, c


def stack_rows(pieces, width):
    index = lax.broadcasted_iota(jnp.int32, (32, width), 0)
    out = jnp.zeros((32, width), F32)
    for k, piece in enumerate(pieces):
        out = jnp.where(index == k, piece, out)
    return out


def source_rows(points, shift):
    norm, hi, lo = features(points, shift, 1.0)
    return stack_rows(hi + lo + hi + lo + [1.0, 1.0, 1.0] + list(split3(norm)), points.shape[1])


def target_rows(points):
    zero = [0.0, 0.0, 0.0]
    norm, hi, lo = features(points, zero, -2.0)
    return stack_rows(hi + hi + lo + lo + list(split3(norm + SOFTENING)) + [1.0, 1.0, 1.0], points.shape[1])


def near_kernel(
    depth, group, q_ref, pb_ref, h_ref, even_ref, odd_ref, nl_ref, pick_a_ref, pick_b_ref,
    basis_ref, t1_ref, t2_ref, k1_ref, k2_ref, coef_ref, top_ref, l1_ref, l2_ref,
    out_ref, cx_ref, yt_ref, rows_ref, w_ref, mask_ref, acc_ref, near_ref,
):
    row, col = lax.axis_index("row"), lax.axis_index("col")
    columns = q_ref.shape[1]
    leaves = columns // 64
    even = row % 2 == 0
    low = lower_half((80, 128))
    lane = lax.broadcasted_iota(jnp.int32, (1, 256), 1)
    for z in range(depth):
        for ye in range(SIDE + 2):
            def piece(k):
                if 1 <= ye <= SIDE:
                    y = ye - 1
                    if k < 2:
                        at = tile_of(z, y, k) * 128
                        return jnp.concatenate([q_ref[:, at : at + 128], pb_ref[:, at : at + 128]], axis=0)
                    at = (z * 4 + y) * 128
                    return h_ref[:, at : at + 128]
                at = (z * 3 + k) * 128
                a, b = even_ref[:, at : at + 128], odd_ref[:, at : at + 128]
                if ye == 0:
                    return jnp.where(even, b, a)
                return jnp.where(even, a, b)

            t0, t1, th = piece(0), piece(1), piece(2)
            for xp, (first, second) in enumerate(((t0, jnp.where(low, t1, th)), (t1, jnp.where(low, th, t0)))):
                cx_ref[xp, z * (SIDE + 2) + ye, :, 0:128] = first[0:64]
                cx_ref[xp, z * (SIDE + 2) + ye, :, 128:256] = second[0:64]
                hl = jnp.concatenate([first[64:80], second[64:80]], axis=1).astype(F32)
                if xp == 0:
                    shift_x = jnp.where(lane >= 192, -float(SIDE), 0.0)
                else:
                    shift_x = jnp.where((lane >= 128) & (lane < 192), float(SIDE), 0.0)
                shift_y = -float(SIDE) if ye == 0 else float(SIDE) if ye == SIDE + 1 else 0.0
                rows_ref[xp, 32 * ye : 32 * ye + 32, :] = source_rows(hl, [shift_x, shift_y, 0.0])
        for xp in range(2):
            for dy in range(3):
                block = rows_ref[xp, 32 * dy : 32 * dy + 128, :]
                yt_ref[xp, dy * depth + z] = block.T.astype(BF16)
    active = jnp.where(nl_ref[...] >= 0, 1.0, 0.0).astype(BF16)
    pick = jnp.where(
        lax.broadcasted_iota(jnp.int32, (48, leaves), 1) % 2 == 0,
        dot(pick_a_ref[...], active, NT),
        dot(pick_b_ref[...], active, NT),
    ).astype(BF16)
    spread = jnp.where(
        lax.broadcasted_iota(jnp.int32, (leaves, columns), 0)
        == lax.broadcasted_iota(jnp.int32, (leaves, columns), 1) // 64,
        1.0,
        0.0,
    ).astype(BF16)
    mask_ref[...] = dot(pick, spread)
    w_ref[...] = jnp.zeros_like(w_ref)

    def target(index, carry):
        tz, xp = index // 2, index % 2
        base = (tz // 4) * 32 + (tz // 2 % 2) * 16 + xp * 4 + (tz % 2) * 2
        for ty in range(SIDE):
            at = pl.multiple_of((base + (ty // 2) * 8 + ty % 2) * 128, 128)
            hl = pb_ref[:, pl.ds(at, 128)].astype(F32)
            w_ref[32 * ty : 32 * ty + 32, 128 * ty : 128 * ty + 128] = target_rows(hl).astype(BF16)
        acc_ref[...] = jnp.zeros_like(acc_ref)

        def layer(dz, carry):
            z = tz + dz - 1
            for dy in range(3):
                left = yt_ref[xp, dy * depth + z]
                for pair in range(2):
                    d2 = dot(left, w_ref[:, 256 * pair : 256 * pair + 256])
                    inv = lax.rsqrt(d2)
                    for half in range(2):
                        ty = 2 * pair + half
                        at = pl.multiple_of((base + (ty // 2) * 8 + ty % 2) * 128, 128)
                        parts = []
                        masks = mask_ref[pl.ds(pl.multiple_of(dz * 16, 16), 16), pl.ds(at, 128)]
                        for k in range(4):
                            m = masks[dy * 4 + k : dy * 4 + k + 1, :]
                            parts.append((inv[64 * k : 64 * k + 64, 128 * half : 128 * half + 128] * m).astype(BF16))
                        kernel = jnp.concatenate(parts, axis=0)
                        acc_ref[ty] += dot(cx_ref[xp, z * (SIDE + 2) + ty + dy], kernel)
            return carry

        lax.fori_loop(jnp.maximum(1 - tz, 0), jnp.minimum(depth + 1 - tz, 3), layer, 0)
        for ty in range(SIDE):
            at = pl.multiple_of((base + (ty // 2) * 8 + ty % 2) * 128, 128)
            near_ref[:, pl.ds(at, 128)] = acc_ref[ty]
        return carry

    lax.fori_loop(0, 2 * depth, target, 0)
    nodes = leaves // 8
    me = row * lax.axis_size("col") + col
    start = row * group
    for m in range(nodes // 8):
        f2 = jnp.zeros((32, 64), F32)
        for s in range(l2_ref.shape[1]):
            v = l2_ref[m, s]
            per = nodes // 8
            at = ((v // per) ^ me) * per + v % per
            f2 = f2 + dot(k2_ref[m, s], top_ref[at])
        hi2, lo2 = split2(f2)
        for n in range(8 * m, 8 * m + 8):
            f1 = dot(t2_ref[32 * n : 32 * n + 32, :], hi2) + dot(t2_ref[32 * n : 32 * n + 32, :], lo2)
            for s in range(l1_ref.shape[1]):
                v = l1_ref[n, s]
                i = jnp.clip(v - start, 0, group - 1)
                at = ((i // nodes) ^ col) * nodes + i % nodes
                term = dot(k1_ref[n, s], coef_ref[at])
                f1 = f1 + jnp.where(v >= 0, term, 0.0)
            hi1, lo1 = split2(f1)
            t1 = t1_ref[256 * n : 256 * n + 256, :]
            leaf = (dot(t1, hi1) + dot(t1, lo1)).astype(BF16)
            chunk = slice(512 * n, 512 * n + 512)
            far = dot(leaf, block_basis(basis_ref[:, chunk]), TN)
            out_ref[:, chunk] = (near_ref[:, chunk] * (NEAR * 64) ** (-0.5) + far).astype(BF16)


def picks():
    a = np.zeros((48, NEAR), np.float32)
    b = np.zeros((48, NEAR), np.float32)
    for dz in range(3):
        for dy in range(3):
            for k in range(4):
                da = (0, 1, None, -1)[k]
                db = (-1, 0, 1, None)[k]
                at = dz * 16 + dy * 4 + k
                if da is not None:
                    a[at, 9 * dz + 3 * dy + da + 1] = 1
                if db is not None:
                    b[at, 9 * dz + 3 * dy + db + 1] = 1
    return jnp.asarray(a, BF16), jnp.asarray(b, BF16)


def doubled(value, axis):
    size = lax.axis_size(axis)
    step = 1
    while step < size:
        other = lax.ppermute(value, axis, [(i, i ^ step) for i in range(size)])
        value = jnp.concatenate([value, other], axis=0)
        step *= 2
    return value


VMEM = pl.BlockSpec(memory_space=pltpu.VMEM)
SMEM = pl.BlockSpec(memory_space=pltpu.SMEM)


def shards(
    charges, points, leaf_basis, transfer_one, transfer_two, couple_one, couple_two, near_list, list_one, list_two
):
    columns = charges.shape[1]
    leaves = near_list.shape[0]
    nodes = leaves // 8
    upper = leaves // 64
    depth = 4 * upper
    rows, cols = lax.axis_size("row"), lax.axis_size("col")
    merge = cols == 2
    t1 = transfer_one.reshape(leaves * 32, 32)
    t2 = transfer_two.reshape(nodes * 32, 32)
    face = jax.ShapeDtypeStruct((80, 2 * depth * 128), BF16)
    params = pltpu.CompilerParams(vmem_limit_bytes=56 * 1024 * 1024)
    outs = pl.pallas_call(
        functools.partial(up_kernel, merge, depth),
        out_shape=[
            jax.ShapeDtypeStruct((16, columns), BF16),
            face,
            jax.ShapeDtypeStruct(((nodes + nodes // 8) * 32, 64), BF16),
        ]
        + ([] if merge else [face]),
        in_specs=[VMEM] * 5,
        out_specs=[VMEM] * (3 if merge else 4),
        compiler_params=params,
        name="up",
    )(charges, points, leaf_basis, t1, t2)
    pb, pay, coef = outs[:3]
    if merge:
        faces = [lax.ppermute(pay, "col", [(0, 1), (1, 0)])]
    else:
        up = [(i, i + 1) for i in range(cols - 1)]
        faces = [
            lax.ppermute(pay, "col", up),
            lax.ppermute(outs[3], "col", [(j, i) for i, j in up]),
        ]
    edge = jax.ShapeDtypeStruct((80, 3 * depth * 128), BF16)
    halo, even, odd = pl.pallas_call(
        functools.partial(pack_kernel, merge, depth),
        out_shape=[jax.ShapeDtypeStruct((80, 4 * depth * 128), BF16), edge, edge],
        in_specs=[VMEM] * (2 + len(faces)),
        out_specs=[VMEM] * 3,
        compiler_params=params,
        name="pack",
    )(charges, pb, *faces)
    even = lax.ppermute(even, "row", [(i, i ^ 1) for i in range(rows)])
    odd = lax.ppermute(odd, "row", [p for i in range(1, rows - 1, 2) for p in ((i, i + 1), (i + 1, i))])
    coef = coef.reshape(1, nodes + nodes // 8, 32, 64)
    coef = doubled(coef, "col")
    ones = coef[:, :nodes].reshape(cols * nodes, 32, 64)
    tops = doubled(coef[:, nodes:].reshape(1, cols * (nodes // 8), 32, 64), "row").reshape(-1, 32, 64)
    pick_a, pick_b = picks()
    return pl.pallas_call(
        functools.partial(near_kernel, depth, cols * nodes),
        out_shape=jax.ShapeDtypeStruct((64, columns), BF16),
        in_specs=[VMEM] * 15 + [SMEM] * 2,
        out_specs=VMEM,
        scratch_shapes=[
            pltpu.VMEM((2, depth * (SIDE + 2), 64, 256), BF16),
            pltpu.VMEM((2, 3 * depth, 256, 128), BF16),
            pltpu.VMEM((2, 32 * (SIDE + 2), 256), F32),
            pltpu.VMEM((128, 512), BF16),
            pltpu.VMEM((48, columns), F32),
            pltpu.VMEM((4, 64, 128), F32),
            pltpu.VMEM((64, columns), F32),
        ],
        compiler_params=params,
        name="near",
    )(
        charges, pb, halo, even, odd, near_list, pick_a, pick_b,
        leaf_basis, t1, t2, couple_one, couple_two, ones, tops, list_one, list_two,
    )


def solution(mesh):
    line, block = P(None, ("row", "col")), P(("row", "col"))
    in_specs = (line, line, line) + (block,) * 7
    return jax.shard_map(shards, mesh=mesh, in_specs=in_specs, out_specs=line, check_vma=False)
```

```python
import functools

import jax
import jax.numpy as jnp
import numpy as np
from jax import lax
from jax.experimental import pallas as pl
from jax.experimental.pallas import tpu as pltpu
from jax.sharding import PartitionSpec as P

NEAR = 27
SIDE = 4
SOFTENING = 0.0025
F32 = jnp.float32
BF16 = jnp.bfloat16
NT = (((1,), (1,)), ((), ()))
TN = (((0,), (0,)), ((), ()))
NN = (((1,), (0,)), ((), ()))
VMEM = pl.BlockSpec(memory_space=pltpu.VMEM)
SMEM = pl.BlockSpec(memory_space=pltpu.SMEM)


def dot(a, b, dims=NN):
    return lax.dot_general(a, b, dims, preferred_element_type=F32)


def split2(v):
    hi = v.astype(BF16)
    lo = (v - hi.astype(F32)).astype(BF16)
    return hi, lo


def tile_of(z, y, x1):
    return (z // 4) * 32 + (z // 2 % 2) * 16 + (y // 2) * 8 + x1 * 4 + (z % 2) * 2 + (y % 2)


def lower_half(shape):
    return lax.broadcasted_iota(jnp.int32, shape, len(shape) - 1) % 128 < 64


def swap_matrix():
    a = lax.broadcasted_iota(jnp.int32, (128, 128), 0)
    b = lax.broadcasted_iota(jnp.int32, (128, 128), 1)
    return jnp.where((a + 64) % 128 == b, 1.0, 0.0).astype(BF16)


def block_basis(basis):
    rank, width = basis.shape
    leaf = lax.broadcasted_iota(jnp.int32, (rank, width), 1) // 64
    zero = jnp.zeros_like(basis)
    return jnp.concatenate([jnp.where(leaf == k, basis, zero) for k in range(8)], axis=0)


def feature_rows(x):
    pairs = [split2(v) for v in x]
    hi = [a.astype(F32) for a, _ in pairs]
    lo = [b.astype(F32) for _, b in pairs]
    y = [a + b for a, b in zip(hi, lo)]
    norm = y[0] * y[0] + y[1] * y[1] + y[2] * y[2]
    n1 = norm.astype(BF16).astype(F32)
    n2 = (norm - n1).astype(BF16).astype(F32)
    n3 = norm - n1 - n2
    width = norm.shape[1]
    index = lax.broadcasted_iota(jnp.int32, (16, width), 0)
    out = jnp.where(index == 9, 1.0, 0.0)
    for k, piece in enumerate(hi + lo + [n1, n2, n3]):
        out = jnp.where(index == k, piece, out)
    return out.astype(BF16)


def with_ones(rows):
    index = lax.broadcasted_iota(jnp.int32, rows.shape, 0)
    return jnp.where(index == 9, jnp.ones_like(rows), rows)


def coordinates(rows):
    return [rows[c : c + 1].astype(F32) + rows[c + 3 : c + 4].astype(F32) for c in range(3)]


def up_kernel(merge, depth, q_ref, pts_ref, basis_ref, t1_ref, t2_ref, feat_ref, xpay_ref, coef_ref, *more):
    row, col = lax.axis_index("row"), lax.axis_index("col")
    columns = q_ref.shape[1]
    nodes = columns // 512
    centre = (
        (SIDE * col + SIDE // 2).astype(F32),
        (SIDE * row + SIDE // 2).astype(F32),
        jnp.float32(depth / 2),
    )
    local = [pts_ref[c : c + 1, :] - centre[c] for c in range(3)]
    feat_ref[...] = feature_rows(local)
    pair_x = lax.broadcasted_iota(jnp.int32, (1, columns), 1) // 512 % 2
    shift = jnp.where(pair_x == 1, -float(SIDE), float(SIDE))
    moved = feature_rows([local[0] + shift, local[1], local[2]])
    swap = swap_matrix()
    low = lower_half((80, 128))
    for z in range(depth):
        for y1 in range(2):
            out = z * 2 + y1

            def tile(y, x1):
                at = tile_of(z, y, x1) * 128
                return jnp.concatenate([q_ref[:, at : at + 128], moved[:, at : at + 128]], axis=0)

            high = jnp.where(low, dot(tile(2 * y1, 1), swap).astype(BF16), tile(2 * y1 + 1, 1))
            base = jnp.where(low, tile(2 * y1, 0), dot(tile(2 * y1 + 1, 0), swap).astype(BF16))
            if merge:
                xpay_ref[:, out * 128 : out * 128 + 128] = jnp.where(col == 0, high, base)
            else:
                xpay_ref[:, out * 128 : out * 128 + 128] = high
                more[0][:, out * 128 : out * 128 + 128] = base
    ones = []
    for n in range(nodes):
        chunk = slice(512 * n, 512 * n + 512)
        leaf = dot(block_basis(basis_ref[:, chunk]), q_ref[:, chunk], NT).astype(BF16)
        ones.append(dot(t1_ref[256 * n : 256 * n + 256, :], leaf, TN).astype(BF16))
    tops = []
    for m in range(nodes // 8):
        part = jnp.concatenate(ones[8 * m : 8 * m + 8], axis=0)
        tops.append(dot(t2_ref[256 * m : 256 * m + 256, :], part, TN).astype(BF16))
    if merge:
        for k in range(nodes // 2):
            coef_ref[32 * k : 32 * k + 32, :] = jnp.concatenate([ones[2 * k], ones[2 * k + 1]], axis=1)
        for m, top in enumerate(tops):
            at = 16 * nodes + 32 * m
            coef_ref[at : at + 32, :] = jnp.concatenate([top, top], axis=1)
        at = 2 * depth * 128
        for k in range(coef_ref.shape[0] // 80):
            xpay_ref[:, at + 128 * k : at + 128 * k + 128] = coef_ref[80 * k : 80 * k + 80, :]
    else:
        for k, value in enumerate(ones + tops):
            coef_ref[32 * k : 32 * k + 32, :] = value


def pack_kernel(merge, depth, q_ref, feat_ref, *refs):
    if merge:
        coef_ref, xr_ref, h_ref, even_ref, odd_ref, one_ref = refs
    else:
        xl_ref, xr_ref, h_ref, even_ref, odd_ref = refs
    row, col = lax.axis_index("row"), lax.axis_index("col")
    swap = swap_matrix()
    low = lower_half((80, 128))
    for z in range(depth):
        for y1 in range(2):
            at = (z * 2 + y1) * 128
            right = xr_ref[:, at : at + 128]
            left = right if merge else xl_ref[:, at : at + 128]
            turned = dot(right, swap).astype(BF16)
            h0 = jnp.where(low, right, turned if merge else dot(left, swap).astype(BF16))
            h1 = jnp.where(low, turned, left)
            at = (z * 4 + 2 * y1) * 128
            h_ref[:, at : at + 128] = h0
            h_ref[:, at + 128 : at + 256] = h1
    even = row % 2 == 0
    for pay, last_first in ((even_ref, even), (odd_ref, jnp.logical_not(even))):
        width = 3 * depth * 128
        for z in range(depth):
            for k in range(3):
                ends = []
                for y in (0, SIDE - 1):
                    if k < 2:
                        at = tile_of(z, y, k) * 128
                        ends.append((q_ref[:, at : at + 128], feat_ref[:, at : at + 128]))
                    else:
                        at = (z * 4 + y) * 128
                        ends.append((h_ref[0:64, at : at + 128], h_ref[64:80, at : at + 128]))
                at = (z * 3 + k) * 128
                pay[0:64, at : at + 128] = jnp.where(last_first, ends[1][0], ends[0][0])
                pay[64:80, at : at + 128] = jnp.where(last_first, ends[1][1], ends[0][1])
        x = coordinates(pay[64:80, 0:width].astype(F32))
        shift = jnp.where(last_first, -float(SIDE), float(SIDE))
        pay[64:80, 0:width] = feature_rows([x[0], x[1] + shift, x[2]])
    if merge:
        nodes = one_ref.shape[0] // 2
        width = 3 * depth * 128
        base = 2 * depth * 128
        got = jnp.concatenate(
            [xr_ref[:, base + 128 * k : base + 128 * k + 128] for k in range(coef_ref.shape[0] // 80)], axis=0
        )
        for side, value in enumerate((coef_ref[...], got)):
            for k in range(nodes // 2):
                block = value[32 * k : 32 * k + 32, :]
                one_ref[side * nodes + 2 * k] = block[:, 0:64]
                one_ref[side * nodes + 2 * k + 1] = block[:, 64:128]
        at = 16 * nodes
        even_ref[:, width : width + 128] = jnp.zeros((80, 128), BF16)
        own, other = coef_ref[at : at + 32, :], got[at : at + 32, :]
        even_ref[0:32, width : width + 128] = jnp.where(lower_half((32, 128)), own, other)


def scan_sources(depth, jobs_of, x_ref, mask_ref, acc_ref):
    def pair(xp, carry):
        add_all([job for sz in range(depth) for job in jobs_of(xp, sz)], depth, xp, x_ref, mask_ref, acc_ref)
        return carry

    lax.fori_loop(0, 2, pair, 0)


def pieces(ye):
    tiles = list(range(max(ye - 2, 0), min(ye, SIDE - 1) + 1))
    return [tiles[k : k + 2] for k in range(0, len(tiles), 2)]


def mask_row(mask_ref, at, dz, dy, k, ty):
    row = dz * 16 + dy * 4 + k
    m = mask_ref[at, row : row + 1, 128 * ty : 128 * ty + 128]
    m = jnp.broadcast_to(m, (16, 128)).astype(BF16)
    return jnp.concatenate([m] * 4, axis=0)


AHEAD = 2


def add_all(jobs, depth, xp, x_ref, mask_ref, acc_ref):
    steps = []
    for sz, ye, tiles, rows, charge, sides in jobs:
        for dz in range(3):
            if 0 <= sz + 1 - dz < depth:
                steps.append((xp * depth + sz + 1 - dz, dz, ye, tiles, rows, charge, sides))
    ready = []
    for i in range(len(steps) + AHEAD):
        if i < len(steps):
            at, dz, ye, tiles, rows, charge, sides = steps[i]
            lanes = slice(128 * tiles[0], 128 * tiles[-1] + 128)
            features = x_ref[at, 32:96, lanes] if sides else x_ref[at, 0:32, lanes]
            ready.append(lax.rsqrt(dot(rows(), features).astype(BF16)))
        if i >= AHEAD:
            at, dz, ye, tiles, rows, charge, sides = steps[i - AHEAD]
            inv = ready[i - AHEAD]
            ready[i - AHEAD] = None
            lanes = slice(128 * tiles[0], 128 * tiles[-1] + 128)
            blocks = []
            for j, ty in enumerate(tiles):
                part = inv[:, 128 * j : 128 * j + 128]
                halves = [part, part] if sides else [part[0:64], part[64:128]]
                first = 2 if sides else 0
                masked = [h * mask_row(mask_ref, at, dz, ye - ty, first + k, ty) for k, h in enumerate(halves)]
                blocks.append(jnp.concatenate(masked, axis=0))
            acc_ref[at, :, lanes] += dot(charge(), jnp.concatenate(blocks, axis=1))


def own_kernel(depth, q_ref, feat_ref, nl_ref, sel_ref, sel_x_ref, pick_ref, acc_ref, x_ref, mask_ref, yt_ref):
    columns = q_ref.shape[1]
    leaves = columns // 64
    x = dot(sel_x_ref[...], feat_ref[...])
    active = jnp.where(nl_ref[...] >= 0, 1.0, 0.0).astype(BF16)
    pick = dot(pick_ref[...], active, NT)
    pick = jnp.where(
        lax.broadcasted_iota(jnp.int32, (48, leaves), 1) % 2 == 0, pick[0:48], pick[48:96]
    ).astype(BF16)
    spread = jnp.where(
        lax.broadcasted_iota(jnp.int32, (leaves, columns), 0)
        == lax.broadcasted_iota(jnp.int32, (leaves, columns), 1) // 64,
        1.0,
        0.0,
    ).astype(BF16)
    masks = dot(pick, spread)
    low = lower_half((32, 128))
    for z in range(depth):
        for xp in range(2):
            for y in range(SIDE):
                at = tile_of(z, y, xp) * 128
                lanes = slice(128 * y, 128 * y + 128)
                tile = x[:, at : at + 128]
                x_ref[xp * depth + z, 0:32, lanes] = tile.astype(BF16)
                x_ref[xp * depth + z, 32:64, lanes] = jnp.where(low, 0.0, tile).astype(BF16)
                x_ref[xp * depth + z, 64:96, lanes] = jnp.where(low, tile, 0.0).astype(BF16)
                mask_ref[xp * depth + z, :, lanes] = masks[:, at : at + 128]
                rows = dot(feat_ref[:, at : at + 128], sel_ref[:, 0:32], TN)
                yt_ref[(xp * depth + z) * SIDE + y] = rows.astype(BF16)
    acc_ref[...] = jnp.zeros_like(acc_ref)

    def jobs_of(xp, sz):
        jobs = []
        for ye in range(1, SIDE + 1):
            base = pl.multiple_of(tile_of(sz, ye - 1, xp) * 128, 128)

            def charge(base=base):
                return q_ref[:, pl.ds(base, 128)]

            def rows(k=(xp * depth + sz) * SIDE + ye - 1):
                return yt_ref[k]

            jobs += [(sz, ye, tiles, rows, charge, False) for tiles in pieces(ye)]
        return jobs

    scan_sources(depth, jobs_of, x_ref, mask_ref, acc_ref)


def beside(right, left):
    return jnp.concatenate([right, left], axis=1)


def side_kernel(depth, q_ref, h_ref, sel_ref, x_ref, mask_ref, yt_ref, in_ref, acc_ref, c_ref, ys_ref):
    low = lower_half((64, 128))
    for z in range(depth):
        for y in range(SIDE):
            t = [q_ref[:, a * 128 : a * 128 + 128] for a in (tile_of(z, y, 0), tile_of(z, y, 1))]
            h = h_ref[:, (z * SIDE + y) * 128 : (z * SIDE + y) * 128 + 128]
            even, odd = z * SIDE + y, (depth + z) * SIDE + y
            c_ref[even] = jnp.where(low, t[1], h[0:64])
            c_ref[odd] = jnp.where(low, h[0:64], t[0])
            rows = dot(with_ones(h[64:80]), sel_ref[:, 0:32], TN).astype(BF16)
            ys_ref[even] = beside(yt_ref[odd, 0:64], rows[64:128])
            ys_ref[odd] = beside(rows[0:64], yt_ref[even, 64:128])

    def jobs_of(xp, sz):
        jobs = []
        for ye in range(1, SIDE + 1):
            k = (xp * depth + sz) * SIDE + ye - 1

            def charge(k=k):
                return c_ref[k]

            def rows(k=k):
                return ys_ref[k]

            jobs += [(sz, ye, tiles, rows, charge, True) for tiles in pieces(ye)]
        return jobs

    scan_sources(depth, jobs_of, x_ref, mask_ref, acc_ref)


def edge_kernel(depth, even_ref, odd_ref, sel_ref, x_ref, mask_ref, in_ref, acc_ref, c_ref, cs_ref, yt_ref, ys_ref):
    even = lax.axis_index("row") % 2 == 0
    low = lower_half((80, 128))
    for z in range(depth):
        for side in range(2):
            t = []
            for k in range(3):
                at = (z * 3 + k) * 128
                a, b = even_ref[:, at : at + 128], odd_ref[:, at : at + 128]
                t.append(jnp.where(even, b, a) if side == 0 else jnp.where(even, a, b))
            rows = [dot(with_ones(v[64:80]), sel_ref[:, 0:32], TN).astype(BF16) for v in t]
            even_k, odd_k = z * 2 + side, (depth + z) * 2 + side
            c_ref[even_k], c_ref[odd_k] = t[0][0:64], t[1][0:64]
            yt_ref[even_k], yt_ref[odd_k] = rows[0], rows[1]
            cs_ref[even_k] = jnp.where(low, t[1], t[2])[0:64]
            cs_ref[odd_k] = jnp.where(low, t[2], t[0])[0:64]
            ys_ref[even_k] = beside(rows[1][0:64], rows[2][64:128])
            ys_ref[odd_k] = beside(rows[2][0:64], rows[0][64:128])

    def jobs_of(xp, sz):
        jobs = []
        for side, ye in enumerate((0, SIDE + 1)):
            k = (xp * depth + sz) * 2 + side
            tiles = [0] if side == 0 else [SIDE - 1]
            for sides, r_ref, q_ref in ((False, yt_ref, c_ref), (True, ys_ref, cs_ref)):

                def charge(q_ref=q_ref, k=k):
                    return q_ref[k]

                def rows(r_ref=r_ref, k=k):
                    return r_ref[k]

                jobs.append((sz, ye, tiles, rows, charge, sides))
        return jobs

    scan_sources(depth, jobs_of, x_ref, mask_ref, acc_ref)


def couple_kernel(group, k1_ref, coef_ref, l1_ref, out_ref):
    row, col = lax.axis_index("row"), lax.axis_index("col")
    nodes, slots = l1_ref.shape
    start = row * group
    for n in range(nodes):
        total = jnp.zeros((32, 64), F32)
        for s in range(slots):
            v = l1_ref[n, s]
            i = jnp.clip(v - start, 0, group - 1)
            at = ((i // nodes) ^ col) * nodes + i % nodes
            partner = coef_ref[at]
            partner = jnp.where(v >= 0, partner, jnp.zeros_like(partner))
            total = total + dot(k1_ref[n, s], partner)
        out_ref[32 * n : 32 * n + 32, :] = total


def down_kernel(depth, wide, acc_ref, f1_ref, basis_ref, t1_ref, t2_ref, k2_ref, top_ref, l2_ref, out_ref, top_scr):
    row, col = lax.axis_index("row"), lax.axis_index("col")
    nodes = out_ref.shape[1] // 512
    per = nodes // 8
    me = row * lax.axis_size("col") + col
    if wide:
        for k in range(top_ref.shape[0]):
            top_scr[2 * k] = top_ref[k][:, 0:64]
            top_scr[2 * k + 1] = top_ref[k][:, 64:128]
    else:
        top_scr[...] = top_ref[...]
    for m in range(per):
        f2 = jnp.zeros((32, 64), F32)
        for s in range(l2_ref.shape[1]):
            v = l2_ref[m, s]
            at = ((v // per) ^ me) * per + v % per
            f2 = f2 + dot(k2_ref[m, s], top_scr[at])
        hi2, lo2 = split2(f2)
        t2 = t2_ref[256 * m : 256 * m + 256, :]
        down = f1_ref[256 * m : 256 * m + 256, :] + dot(t2, hi2) + dot(t2, lo2)
        hi1, lo1 = split2(down)
        for j in range(8):
            n = 8 * m + j
            t1 = t1_ref[256 * n : 256 * n + 256, :]
            rows = slice(32 * j, 32 * j + 32)
            leaf = (dot(t1, hi1[rows]) + dot(t1, lo1[rows])).astype(BF16)
            chunk = slice(512 * n, 512 * n + 512)
            far = dot(leaf, block_basis(basis_ref[:, chunk]), TN)
            z1, y1, x1 = j // 4, j // 2 % 2, j % 2
            for k in range(4):
                z, y = 4 * m + 2 * z1 + k // 2, 2 * y1 + k % 2
                part = acc_ref[x1 * depth + z, :, 128 * y : 128 * y + 128]
                total = part * (NEAR * 64) ** (-0.5) + far[:, 128 * k : 128 * k + 128]
                out_ref[:, 512 * n + 128 * k : 512 * n + 128 * k + 128] = total.astype(BF16)


def constants():
    sel = np.zeros((16, 160), np.float32)
    sel_x = np.zeros((32, 16), np.float32)
    rest, eps = np.float32(SOFTENING), []
    for _ in range(3):
        eps.append(np.asarray(rest).astype(jnp.bfloat16).astype(np.float32))
        rest = np.float32(rest - eps[-1])
    for f in range(21):
        source = f if f < 6 else f - 6 if f < 12 else 9 if f < 15 else f - 9 if f < 18 else 9
        for base in (0, 32, 128):
            sel[source, base + f] = 1
        if f < 12:
            sel_x[f, f % 3 + (3 if f >= 6 else 0)] = -2
        elif f < 15:
            sel_x[f, f - 6] = 1
        else:
            sel_x[f, 9] = 1 if f < 18 else eps[f - 18]
    pick = np.zeros((96, NEAR), np.float32)
    for dz in range(3):
        for dy in range(3):
            for k in range(4):
                for half, dx in enumerate(((0, 1, None, -1)[k], (-1, 0, 1, None)[k])):
                    if dx is not None:
                        pick[48 * half + dz * 16 + dy * 4 + k, 9 * dz + 3 * dy + dx + 1] = 1
    return [jnp.asarray(v, BF16) for v in (sel, sel_x, pick)]


def doubled(value, axis, start=1):
    size = lax.axis_size(axis)
    step = start
    while step < size:
        other = lax.ppermute(value, axis, [(i, i ^ step) for i in range(size)])
        value = jnp.concatenate([value, other], axis=0)
        step *= 2
    return value


def call(kernel, name, out_shape, ins, smem=0, scratch=(), flops=0, alias=None):
    single = not isinstance(out_shape, list)
    return pl.pallas_call(
        kernel,
        out_shape=out_shape,
        in_specs=[VMEM] * (len(ins) - smem) + [SMEM] * smem,
        out_specs=VMEM if single else [VMEM] * len(out_shape),
        scratch_shapes=list(scratch),
        input_output_aliases={alias: 0} if alias is not None else {},
        compiler_params=pltpu.CompilerParams(vmem_limit_bytes=40 * 1024 * 1024),
        cost_estimate=pl.CostEstimate(flops=flops, bytes_accessed=1 << 20, transcendentals=0) if flops else None,
        name=name,
    )(*ins)


def shards(
    charges, points, leaf_basis, transfer_one, transfer_two, couple_one, couple_two, near_list, list_one, list_two
):
    columns = charges.shape[1]
    leaves = near_list.shape[0]
    nodes = leaves // 8
    tops = nodes // 8
    depth = 4 * (leaves // 64)
    rows, cols = lax.axis_size("row"), lax.axis_size("col")
    merge = cols == 2 and tops == 1
    t1 = transfer_one.reshape(leaves * 32, 32)
    t2 = transfer_two.reshape(nodes * 32, 32)
    shape = jax.ShapeDtypeStruct
    face = 2 * depth * 128
    outs = call(
        functools.partial(up_kernel, merge, depth),
        "up",
        [shape((16, columns), BF16)]
        + (
            [shape((80, face + 256), BF16), shape((16 * nodes + 32, 128), BF16)]
            if merge
            else [shape((80, face), BF16), shape(((nodes + tops) * 32, 64), BF16), shape((80, face), BF16)]
        ),
        [charges, points, leaf_basis, t1, t2],
    )
    feat, pay, coef = outs[:3]
    if merge:
        faces = [coef, lax.ppermute(pay, "col", [(0, 1), (1, 0)])]
    else:
        up = [(i, i + 1) for i in range(cols - 1)]
        faces = [lax.ppermute(pay, "col", up), lax.ppermute(outs[3], "col", [(j, i) for i, j in up])]
    sel, sel_x, pick = constants()
    acc_shape = shape((2 * depth, 64, 512), F32)
    acc, x, mask, yt = call(
        functools.partial(own_kernel, depth),
        "own",
        [
            acc_shape,
            shape((2 * depth, 96, 512), BF16),
            shape((2 * depth, 48, 512), F32),
            shape((2 * depth * SIDE, 128, 32), BF16),
        ],
        [charges, feat, near_list, sel, sel_x, pick],
        flops=1 << 32,
    )
    edge = 3 * depth * 128
    packed = call(
        functools.partial(pack_kernel, merge, depth),
        "pack",
        [
            shape((80, 4 * depth * 128), BF16),
            shape((80, edge + (128 if merge else 0)), BF16),
            shape((80, edge), BF16),
        ]
        + ([shape((2 * nodes, 32, 64), BF16)] if merge else []),
        [charges, feat, *faces],
    )
    halo, even, odd = packed[:3]
    mine = even
    even = lax.ppermute(even, "row", [(i, i ^ 1) for i in range(rows)])
    odd = lax.ppermute(odd, "row", [p for i in range(1, rows - 1, 2) for p in ((i, i + 1), (i + 1, i))])
    acc = call(
        functools.partial(side_kernel, depth),
        "side",
        acc_shape,
        [charges, halo, sel, x, mask, yt, acc],
        alias=6,
        scratch=[pltpu.VMEM((2 * depth * SIDE, 64, 128), BF16), pltpu.VMEM((2 * depth * SIDE, 64, 64), BF16)],
        flops=1 << 32,
    )
    if merge:
        one = packed[3]
        top = jnp.stack([mine[0:32, edge:], even[0:32, edge:]])
        top = doubled(top, "row", 2)
    else:
        coef = doubled(coef.reshape(1, nodes + tops, 32, 64), "col")
        one = coef[:, :nodes].reshape(cols * nodes, 32, 64)
        top = doubled(coef[:, nodes:].reshape(1, cols * tops, 32, 64), "row").reshape(-1, 32, 64)
    field = call(
        functools.partial(couple_kernel, cols * nodes),
        "couple",
        shape((nodes * 32, 64), F32),
        [couple_one, one, list_one],
        smem=1,
        flops=1 << 30,
    )
    small = [pltpu.VMEM((4 * depth, 64, 128), BF16), pltpu.VMEM((4 * depth, 64, 128), BF16)]
    acc = call(
        functools.partial(edge_kernel, depth),
        "edge",
        acc_shape,
        [even, odd, sel, x, mask, acc],
        alias=5,
        scratch=small + [pltpu.VMEM((4 * depth, 128, 32), BF16), pltpu.VMEM((4 * depth, 64, 64), BF16)],
        flops=1 << 31,
    )
    return call(
        functools.partial(down_kernel, depth, merge),
        "down",
        shape((64, columns), BF16),
        [acc, field, leaf_basis, t1, t2, couple_two, top, list_two],
        smem=1,
        scratch=[pltpu.VMEM((rows * cols * tops, 32, 64), BF16)],
    )


def solution(mesh):
    line, block = P(None, ("row", "col")), P(("row", "col"))
    in_specs = (line, line, line) + (block,) * 7
    return jax.shard_map(shards, mesh=mesh, in_specs=in_specs, out_specs=line, check_vma=False)
```

```python
import functools

import jax
import jax.numpy as jnp
import numpy as np
from jax import lax
from jax.experimental import pallas as pl
from jax.experimental.pallas import tpu as pltpu
from jax.sharding import PartitionSpec as P


NEAR = 27
SIDE = 4
SOFTENING = 0.0025
F32 = jnp.float32
BF16 = jnp.bfloat16
NT = (((1,), (1,)), ((), ()))
TN = (((0,), (0,)), ((), ()))
NN = (((1,), (0,)), ((), ()))
VMEM = pl.BlockSpec(memory_space=pltpu.VMEM)
SMEM = pl.BlockSpec(memory_space=pltpu.SMEM)
HBM = pl.BlockSpec(memory_space=pltpu.MemorySpace.HBM)


def dot(a, b, dims=NN):
    return lax.dot_general(a, b, dims, preferred_element_type=F32)


def split2(v):
    hi = v.astype(BF16)
    lo = (v - hi.astype(F32)).astype(BF16)
    return hi, lo


def tile_of(z, y, x1):
    return (z // 4) * 32 + (z // 2 % 2) * 16 + (y // 2) * 8 + x1 * 4 + (z % 2) * 2 + (y % 2)


def lower_half(shape):
    return lax.broadcasted_iota(jnp.int32, shape, len(shape) - 1) % 128 < 64


def swap_matrix():
    a = lax.broadcasted_iota(jnp.int32, (128, 128), 0)
    b = lax.broadcasted_iota(jnp.int32, (128, 128), 1)
    return jnp.where((a + 64) % 128 == b, 1.0, 0.0).astype(BF16)


def block_basis(basis):
    rank, width = basis.shape
    leaf = lax.broadcasted_iota(jnp.int32, (rank, width), 1) // 64
    zero = jnp.zeros_like(basis)
    return jnp.concatenate([jnp.where(leaf == k, basis, zero) for k in range(8)], axis=0)


def feature_rows(x):
    pairs = [split2(v) for v in x]
    hi = [a.astype(F32) for a, _ in pairs]
    lo = [b.astype(F32) for _, b in pairs]
    y = [a + b for a, b in zip(hi, lo)]
    norm = y[0] * y[0] + y[1] * y[1] + y[2] * y[2]
    n1 = norm.astype(BF16).astype(F32)
    n2 = (norm - n1).astype(BF16).astype(F32)
    n3 = norm - n1 - n2
    width = norm.shape[1]
    index = lax.broadcasted_iota(jnp.int32, (16, width), 0)
    out = jnp.where(index == 9, 1.0, 0.0)
    for k, piece in enumerate(hi + lo + [n1, n2, n3]):
        out = jnp.where(index == k, piece, out)
    return out.astype(BF16)


def with_ones(rows):
    index = lax.broadcasted_iota(jnp.int32, rows.shape, 0)
    return jnp.where(index == 9, jnp.ones_like(rows), rows)


def coordinates(rows):
    return [rows[c : c + 1].astype(F32) + rows[c + 3 : c + 4].astype(F32) for c in range(3)]


def swapped(tiles):
    out = dot(jnp.concatenate(tiles, axis=0), swap_matrix()).astype(BF16)
    size = tiles[0].shape[0]
    return [out[size * k : size * k + size] for k in range(len(tiles))]


def halves(firsts, seconds, x1):
    low = lower_half(firsts[0].shape)
    if x1 == 1:
        return [jnp.where(low, a, b) for a, b in zip(swapped(firsts), seconds)]
    return [jnp.where(low, a, b) for a, b in zip(firsts, swapped(seconds))]


def unpacked(rights, lefts):
    low = lower_half(rights[0].shape)
    turned = swapped(rights)
    other = turned if rights is lefts else swapped(lefts)
    return [
        (jnp.where(low, r, o), jnp.where(low, t, l)) for r, l, t, o in zip(rights, lefts, turned, other)
    ]


def tiles_in(ref, first, count):
    return [ref[:, 128 * k : 128 * k + 128] for k in range(first, first + count)]


def transposed(tiles, sel_ref):
    rows = dot(jnp.concatenate(tiles, axis=1), sel_ref[:, 0:32], TN).astype(BF16)
    return [rows[128 * k : 128 * k + 128] for k in range(len(tiles))]


def send_rows(pay_ref, last_first, q_ref, feat, depth):
    width = 2 * depth * 128
    for z in range(depth):
        for k in range(2):
            ats = [tile_of(z, y, k) * 128 for y in (SIDE - 1, 0)]
            at = (z * 2 + k) * 128
            pay_ref[0:64, at : at + 128] = jnp.where(
                last_first, q_ref[:, ats[0] : ats[0] + 128], q_ref[:, ats[1] : ats[1] + 128]
            )
            pay_ref[64:80, at : at + 128] = jnp.where(
                last_first, feat[:, ats[0] : ats[0] + 128], feat[:, ats[1] : ats[1] + 128]
            )
    x = coordinates(pay_ref[64:80, 0:width].astype(F32))
    shift = jnp.where(last_first, -float(SIDE), float(SIDE))
    pay_ref[64:80, 0:width] = feature_rows([x[0], x[1] + shift, x[2]])


def face_kernel(merge, depth, q_hbm, pts_hbm, q_ref, feat_ref, odd_ref, xpay_ref, *more):
    pts_ref, sems = more[-2:]
    copies = [
        pltpu.make_async_copy(pts_hbm, pts_ref, sems.at[0]),
        pltpu.make_async_copy(q_hbm, q_ref, sems.at[1]),
    ]
    for copy in copies:
        copy.start()
    row, col = lax.axis_index("row"), lax.axis_index("col")
    columns = q_ref.shape[1]
    centre = (
        (SIDE * col + SIDE // 2).astype(F32),
        (SIDE * row + SIDE // 2).astype(F32),
        jnp.float32(depth / 2),
    )
    copies[0].wait()
    local = [pts_ref[c : c + 1, :] - centre[c] for c in range(3)]
    feat = feature_rows(local)
    feat_ref[...] = feat
    pair_x = lax.broadcasted_iota(jnp.int32, (1, columns), 1) // 512 % 2
    shift = jnp.where(pair_x == 1, -float(SIDE), float(SIDE))
    moved = feature_rows([local[0] + shift, local[1], local[2]])
    copies[1].wait()

    def tile(z, y, x1):
        at = tile_of(z, y, x1) * 128
        return jnp.concatenate([q_ref[:, at : at + 128], moved[:, at : at + 128]], axis=0)

    places = [(z, y1) for z in range(depth) for y1 in range(2)]
    sides = [[[tile(z, 2 * y1 + k, x1) for z, y1 in places] for k in range(2)] for x1 in range(2)]
    if merge:
        first = [jnp.where(col == 0, a, b) for a, b in zip(sides[1][0], sides[0][1])]
        second = [jnp.where(col == 0, a, b) for a, b in zip(sides[1][1], sides[0][0])]
        low = lower_half((80, 128)) == (col == 0)
        for k, (a, b) in enumerate(zip(swapped(first), second)):
            xpay_ref[:, 128 * k : 128 * k + 128] = jnp.where(low, a, b)
    else:
        for ref, x1 in ((xpay_ref, 1), (more[0], 0)):
            for k, value in enumerate(halves(*sides[x1], x1)):
                ref[:, 128 * k : 128 * k + 128] = value
    send_rows(odd_ref, row % 2 == 1, q_ref, feat, depth)


def up_kernel(merge, depth, q_ref, feat_ref, basis_ref, t1_ref, t2_ref, even_ref, coef_ref):
    nodes = q_ref.shape[1] // 512
    leaf = []
    for n in range(nodes):
        chunk = slice(512 * n, 512 * n + 512)
        leaf.append(dot(block_basis(basis_ref[:, chunk]), q_ref[:, chunk], NT).astype(BF16))
    ones = [dot(t1_ref[256 * n : 256 * n + 256, :], leaf[n], TN).astype(BF16) for n in range(nodes)]
    tops = []
    for m in range(nodes // 8):
        part = jnp.concatenate(ones[8 * m : 8 * m + 8], axis=0)
        tops.append(dot(t2_ref[256 * m : 256 * m + 256, :], part, TN).astype(BF16))
    send_rows(even_ref, lax.axis_index("row") % 2 == 0, q_ref, feat_ref, depth)
    if merge:
        for k in range(nodes // 2):
            coef_ref[32 * k : 32 * k + 32, :] = jnp.concatenate([ones[2 * k], ones[2 * k + 1]], axis=1)
        both = jnp.concatenate([tops[0], tops[0]], axis=1)
        coef_ref[16 * nodes : 16 * nodes + 32, :] = both
        width = 2 * depth * 128
        even_ref[0:32, width : width + 128] = both
        even_ref[32:80, width : width + 128] = jnp.zeros((48, 128), BF16)
    else:
        for k, value in enumerate(ones + tops):
            coef_ref[32 * k : 32 * k + 32, :] = value


def row_sides(even_ref, odd_ref):
    even = lax.axis_index("row") % 2 == 0

    def face(side, at):
        a, b = even_ref[:, at : at + 128], odd_ref[:, at : at + 128]
        return jnp.where(even, b, a) if side == 0 else jnp.where(even, a, b)

    return face


def corner_kernel(merge, depth, even_ref, odd_ref, *refs):
    col = lax.axis_index("col")
    face = row_sides(even_ref, odd_ref)
    coef_ref, pay_ref = refs if merge else (None, refs[0])
    tiles = [[[face(side, (z * 2 + k) * 128) for z in range(depth)] for side in range(2)] for k in range(2)]
    high, base = halves(*tiles[1], 1), halves(*tiles[0], 0)
    groups = [(pay_ref, jnp.concatenate(high, axis=1), -float(SIDE))]
    if merge:
        mine = jnp.where(col == 0, groups[0][1], jnp.concatenate(base, axis=1))
        groups = [(pay_ref, mine, jnp.where(col == 0, -float(SIDE), float(SIDE)))]
    else:
        groups.append((refs[1], jnp.concatenate(base, axis=1), float(SIDE)))
    width = depth * 128
    for ref, tile, shift in groups:
        ref[0:64, 0:width] = tile[0:64]
        x = coordinates(tile[64:80].astype(F32))
        ref[64:80, 0:width] = feature_rows([x[0] + shift, x[1], x[2]])
    if merge:
        rest = coef_ref.shape[0] - 32
        other = even_ref[0:32, 2 * depth * 128 : 2 * depth * 128 + 128]
        tops = jnp.where(lower_half((32, 128)), coef_ref[rest : rest + 32, :], other)
        blocks = jnp.concatenate([coef_ref[0:rest, :], tops], axis=0)
        for k in range(blocks.shape[0] // 80):
            pay_ref[:, width + 128 * k : width + 128 * k + 128] = blocks[80 * k : 80 * k + 80]


def layers_of(depth, tz):
    return [sz for sz in (tz - 1, tz, tz + 1) if 0 <= sz < depth]


def inner_steps(depth):
    steps = []
    for tz in range(depth):
        layers = layers_of(depth, tz)
        for sz in layers:
            steps.append((tz, (0, 1), [(sz, 1), (sz, 2)]))
            steps.append((tz, (2, 3), [(sz, 3), (sz, 4)]))
        steps.append((tz, (1,), [(sz, 3) for sz in layers]))
        steps.append((tz, (2,), [(sz, 2) for sz in layers]))
    return steps


def mask_row(mask_ref, at, dz, dy, k, ty):
    row = dz * 16 + dy * 4 + k
    m = mask_ref[at, row : row + 1, 128 * ty : 128 * ty + 128]
    m = jnp.broadcast_to(m, (16, 128)).astype(BF16)
    return jnp.concatenate([m] * 4, axis=0)


AHEAD = 6


def scan(steps, depth, rows_of, charge_of, x_ref, mask_ref, acc_ref, fresh=False):
    def pair(xp, carry):
        ready, seen = [], set()
        for i in range(len(steps) + AHEAD):
            if i < len(steps):
                sides, (tz, tiles, sources) = steps[i]
                lanes = slice(128 * tiles[0], 128 * tiles[-1] + 128)
                at = xp * depth + tz
                rows = jnp.concatenate([rows_of(sides, xp, sz, ye) for sz, ye in sources], axis=0)
                features = x_ref[at, 32:96, lanes] if sides else x_ref[at, 0:32, lanes]
                ready.append(lax.rsqrt(dot(rows, features).astype(BF16)))
            if i >= AHEAD:
                sides, (tz, tiles, sources) = steps[i - AHEAD]
                inv, ready[i - AHEAD] = ready[i - AHEAD], None
                lanes = slice(128 * tiles[0], 128 * tiles[-1] + 128)
                at = xp * depth + tz
                size = 64 if sides else 128
                columns = []
                for j, ty in enumerate(tiles):
                    blocks = []
                    for k, (sz, ye) in enumerate(sources):
                        part = inv[size * k : size * k + size, 128 * j : 128 * j + 128]
                        halves = [part, part] if sides else [part[0:64], part[64:128]]
                        first = 2 if sides else 0
                        blocks += [
                            h * mask_row(mask_ref, at, sz - tz + 1, ye - ty, first + c, ty) for c, h in enumerate(halves)
                        ]
                    columns.append(jnp.concatenate(blocks, axis=0))
                kernel = columns[0] if len(columns) == 1 else jnp.concatenate(columns, axis=1)
                charge = jnp.concatenate([charge_of(sides, xp, sz, ye) for sz, ye in sources], axis=1)
                value = dot(charge, kernel)
                if fresh and len(tiles) == 2 and (tz, tiles) not in seen:
                    seen.add((tz, tiles))
                    acc_ref[at, :, lanes] = value
                else:
                    acc_ref[at, :, lanes] += value
        return carry

    lax.fori_loop(0, 2, pair, 0)


def own_kernel(depth, q_ref, feat_ref, nl_ref, sel_ref, sel_x_ref, pick_ref, acc_ref, x_ref, mask_ref, yt_ref):
    columns = q_ref.shape[1]
    leaves = columns // 64
    x = dot(sel_x_ref[...], feat_ref[...])
    active = jnp.where(nl_ref[...] >= 0, 1.0, 0.0).astype(BF16)
    pick = dot(pick_ref[...], active)
    pick = jnp.where(
        lax.broadcasted_iota(jnp.int32, (48, leaves), 1) % 2 == 0, pick[0:48], pick[48:96]
    ).astype(BF16)
    spread = jnp.where(
        lax.broadcasted_iota(jnp.int32, (leaves, columns), 0)
        == lax.broadcasted_iota(jnp.int32, (leaves, columns), 1) // 64,
        1.0,
        0.0,
    ).astype(BF16)
    masks = dot(pick, spread)
    low = lower_half((32, 128))
    rows = dot(feat_ref[...], sel_ref[:, 0:32], TN).astype(BF16)
    for z in range(depth):
        for xp in range(2):
            for y in range(SIDE):
                at = tile_of(z, y, xp) * 128
                lanes = slice(128 * y, 128 * y + 128)
                tile = x[:, at : at + 128]
                x_ref[xp * depth + z, 0:32, lanes] = tile.astype(BF16)
                x_ref[xp * depth + z, 32:64, lanes] = jnp.where(low, 0.0, tile).astype(BF16)
                x_ref[xp * depth + z, 64:96, lanes] = jnp.where(low, tile, 0.0).astype(BF16)
                mask_ref[xp * depth + z, :, lanes] = masks[:, at : at + 128]
                yt_ref[(xp * depth + z) * SIDE + y] = rows[at : at + 128]

    def rows_of(sides, xp, sz, ye):
        return yt_ref[(xp * depth + sz) * SIDE + ye - 1]

    def charge_of(sides, xp, sz, ye):
        base = pl.multiple_of(tile_of(sz, ye - 1, xp) * 128, 128)
        return q_ref[:, pl.ds(base, 128)]

    steps = [(False, step) for step in inner_steps(depth)]
    scan(steps, depth, rows_of, charge_of, x_ref, mask_ref, acc_ref, fresh=True)


def beside(right, left):
    return jnp.concatenate([right, left], axis=1)


def side_kernel(merge, depth, q_ref, right_ref, *refs):
    if not merge:
        left_ref, *refs = refs
    sel_ref, x_ref, mask_ref, yt_ref, _, acc_ref, c_ref, ys_ref = refs
    low = lower_half((64, 128))
    count = right_ref.shape[1] // 128
    rights = tiles_in(right_ref, 0, count)
    lefts = rights if merge else tiles_in(left_ref, 0, count)
    beyond = [tile for pair in unpacked(rights, lefts) for tile in pair]
    turned = transposed([with_ones(h[64:80]) for h in beyond], sel_ref)
    for z in range(depth):
        for y in range(SIDE):
            t = [q_ref[:, a * 128 : a * 128 + 128] for a in (tile_of(z, y, 0), tile_of(z, y, 1))]
            even, odd = z * SIDE + y, (depth + z) * SIDE + y
            h, rows = beyond[even][0:64], turned[even]
            c_ref[even] = jnp.where(low, t[1], h)
            c_ref[odd] = jnp.where(low, h, t[0])
            ys_ref[even] = beside(yt_ref[odd, 0:64], rows[64:128])
            ys_ref[odd] = beside(rows[0:64], yt_ref[even, 64:128])

    def rows_of(sides, xp, sz, ye):
        return ys_ref[(xp * depth + sz) * SIDE + ye - 1]

    def charge_of(sides, xp, sz, ye):
        return c_ref[(xp * depth + sz) * SIDE + ye - 1]

    scan([(True, step) for step in inner_steps(depth)], depth, rows_of, charge_of, x_ref, mask_ref, acc_ref)


def edge_steps(depth, sides):
    steps = []
    for tz in range(depth):
        for side in range(2):
            sources = [(sz, side * (SIDE + 1)) for sz in layers_of(depth, tz)]
            steps.append((sides, (tz, (side * (SIDE - 1),), sources)))
    return steps


def edge_kernel(depth, even_ref, odd_ref, sel_ref, x_ref, mask_ref, in_ref, acc_ref, c_ref, yt_ref):
    face = row_sides(even_ref, odd_ref)
    places = [(k, z, side) for k in range(2) for z in range(depth) for side in range(2)]
    tiles = [face(side, (z * 2 + k) * 128) for k, z, side in places]
    for i, rows in enumerate(transposed([with_ones(tile[64:80]) for tile in tiles], sel_ref)):
        c_ref[i] = tiles[i][0:64]
        yt_ref[i] = rows

    def rows_of(sides, xp, sz, ye):
        return yt_ref[(xp * depth + sz) * 2 + (ye > 0)]

    def charge_of(sides, xp, sz, ye):
        return c_ref[(xp * depth + sz) * 2 + (ye > 0)]

    scan(edge_steps(depth, False), depth, rows_of, charge_of, x_ref, mask_ref, acc_ref)


def last_kernel(merge, depth, edge_c_ref, edge_y_ref, right_ref, *refs):
    if not merge:
        left_ref, *refs = refs
    sel_ref, x_ref, mask_ref, _, acc_ref, c_ref, ys_ref = refs
    low = lower_half((64, 128))
    rights = tiles_in(right_ref, 0, depth)
    lefts = rights if merge else tiles_in(left_ref, 0, depth)
    beyond = [tile for pair in unpacked(rights, lefts) for tile in pair]
    turned = transposed([with_ones(h[64:80]) for h in beyond], sel_ref)
    for z in range(depth):
        for side in range(2):
            even, odd = z * 2 + side, (depth + z) * 2 + side
            h, rows = beyond[even][0:64], turned[even]
            c_ref[even] = jnp.where(low, edge_c_ref[odd], h)
            c_ref[odd] = jnp.where(low, h, edge_c_ref[even])
            ys_ref[even] = beside(edge_y_ref[odd, 0:64], rows[64:128])
            ys_ref[odd] = beside(rows[0:64], edge_y_ref[even, 64:128])

    def rows_of(sides, xp, sz, ye):
        return ys_ref[(xp * depth + sz) * 2 + (ye > 0)]

    def charge_of(sides, xp, sz, ye):
        return c_ref[(xp * depth + sz) * 2 + (ye > 0)]

    scan(edge_steps(depth, True), depth, rows_of, charge_of, x_ref, mask_ref, acc_ref)


def couple_kernel(merge, group, k1_ref, *refs):
    col = lax.axis_index("col")
    if merge:
        own_ref, got_ref, l1_ref, out_ref, coef_ref = refs
        nodes = l1_ref.shape[0]
        at = got_ref.shape[1] - 256
        got = jnp.concatenate([got_ref[:, at : at + 128], got_ref[:, at + 128 : at + 256]], axis=0)
        for k in range(nodes // 2):
            for side, value in enumerate((own_ref[32 * k : 32 * k + 32, :], got[32 * k : 32 * k + 32])):
                coef_ref[side * nodes + 2 * k] = value[:, 0:64]
                coef_ref[side * nodes + 2 * k + 1] = value[:, 64:128]
        coef_ref[group] = jnp.zeros((32, 64), BF16)
    else:
        coef_ref, l1_ref, out_ref = refs
    nodes, slots = l1_ref.shape
    mask = col * nodes
    zero = jnp.zeros((32, 64), BF16)
    totals = []
    for n in range(nodes):
        parts = []
        for s in range(slots):
            v = l1_ref[n, s]
            at = (v & (group - 1)) ^ mask
            if merge:
                parts.append(coef_ref[jnp.where(v >= 0, at, group)])
            else:
                parts.append(jnp.where(v >= 0, coef_ref[at], zero))
        matrix = jnp.concatenate([k1_ref[n, s] for s in range(slots)], axis=1)
        totals.append(dot(matrix, jnp.concatenate(parts, axis=0)))
    for n in range(nodes):
        out_ref[32 * n : 32 * n + 32, :] = totals[n]


def down_kernel(depth, wide, acc_ref, f1_ref, basis_ref, t1_ref, t2_ref, k2_ref, top_ref, l2_ref, out_hbm, *refs):
    out_ref, sems, top_scr = refs
    row, col = lax.axis_index("row"), lax.axis_index("col")
    nodes = out_hbm.shape[1] // 512
    per = nodes // 8
    me = row * lax.axis_size("col") + col
    if wide:
        for k in range(top_ref.shape[0]):
            top_scr[(k // 2) * 4 + k % 2] = top_ref[k, :, 0:64]
            top_scr[(k // 2) * 4 + 2 + k % 2] = top_ref[k, :, 64:128]
    else:
        top_scr[...] = top_ref[...]
    copies = []
    for m in range(per):
        parts = []
        for s in range(l2_ref.shape[1]):
            v = l2_ref[m, s]
            at = v ^ me if per == 1 else ((v // per) ^ me) * per + v % per
            parts.append(top_scr[at])
        matrix = jnp.concatenate([k2_ref[m, s] for s in range(l2_ref.shape[1])], axis=1)
        hi2, lo2 = split2(dot(matrix, jnp.concatenate(parts, axis=0)))
        t2 = t2_ref[256 * m : 256 * m + 256, :]
        hi1, lo1 = split2(f1_ref[256 * m : 256 * m + 256, :] + dot(t2, hi2) + dot(t2, lo2))
        leaves = []
        for j in range(8):
            n = 8 * m + j
            t1 = t1_ref[256 * n : 256 * n + 256, :]
            rows = slice(32 * j, 32 * j + 32)
            leaves.append((dot(t1, hi1[rows]) + dot(t1, lo1[rows])).astype(BF16))
        for j in range(8):
            n = 8 * m + j
            far = dot(leaves[j], block_basis(basis_ref[:, 512 * n : 512 * n + 512]), TN)
            z1, y1, x1 = j // 4, j // 2 % 2, j % 2
            for k in range(4):
                z, y = 4 * m + 2 * z1 + k // 2, 2 * y1 + k % 2
                part = acc_ref[x1 * depth + z, :, 128 * y : 128 * y + 128]
                total = part * (NEAR * 64) ** (-0.5) + far[:, 128 * k : 128 * k + 128]
                out_ref[:, 512 * n + 128 * k : 512 * n + 128 * k + 128] = total.astype(BF16)
            lanes = pl.ds(512 * n, 512)
            copies.append(pltpu.make_async_copy(out_ref.at[:, lanes], out_hbm.at[:, lanes], sems.at[n]))
            copies[-1].start()
    for copy in copies:
        copy.wait()


def constants():
    sel = np.zeros((16, 160), np.float32)
    sel_x = np.zeros((32, 16), np.float32)
    rest, eps = np.float32(SOFTENING), []
    for _ in range(3):
        eps.append(np.asarray(rest).astype(jnp.bfloat16).astype(np.float32))
        rest = np.float32(rest - eps[-1])
    for f in range(21):
        source = f if f < 6 else f - 6 if f < 12 else 9 if f < 15 else f - 9 if f < 18 else 9
        for base in (0, 32, 128):
            sel[source, base + f] = 1
        if f < 12:
            sel_x[f, f % 3 + (3 if f >= 6 else 0)] = -2
        elif f < 15:
            sel_x[f, f - 6] = 1
        else:
            sel_x[f, 9] = 1 if f < 18 else eps[f - 18]
    pick = np.zeros((96, NEAR), np.float32)
    for dz in range(3):
        for dy in range(3):
            for k in range(4):
                for half, dx in enumerate(((0, 1, None, -1)[k], (-1, 0, 1, None)[k])):
                    if dx is not None:
                        pick[48 * half + dz * 16 + dy * 4 + k, 9 * dz + 3 * dy + dx + 1] = 1
    return [jnp.asarray(v, BF16) for v in (sel, sel_x, pick)]


def doubled(value, axis, start=1):
    size = lax.axis_size(axis)
    step = start
    while step < size:
        other = lax.ppermute(value, axis, [(i, i ^ step) for i in range(size)])
        value = jnp.concatenate([value, other], axis=0)
        step *= 2
    return value


def call(kernel, out_shape, ins, smem=0, scratch=(), flops=0, alias=None, hbm_in=0, hbm_out=False):
    single = not isinstance(out_shape, list)
    return pallas(kernel, out_shape, ins, smem, scratch, flops, alias, single, hbm_in, hbm_out)


def pallas(kernel, out_shape, ins, smem, scratch, flops, alias, single, hbm_in, hbm_out):
    return pl.pallas_call(
        kernel,
        out_shape=out_shape,
        in_specs=[HBM] * hbm_in + [VMEM] * (len(ins) - smem - hbm_in) + [SMEM] * smem,
        out_specs=(HBM if hbm_out else VMEM) if single else [VMEM] * len(out_shape),
        scratch_shapes=list(scratch),
        input_output_aliases={alias: 0} if alias is not None else {},
        compiler_params=pltpu.CompilerParams(vmem_limit_bytes=40 * 1024 * 1024),
        cost_estimate=pl.CostEstimate(flops=flops, bytes_accessed=1 << 20, transcendentals=0) if flops else None,
    )(*ins)


def shards(
    charges, points, leaf_basis, transfer_one, transfer_two, couple_one, couple_two, near_list, list_one, list_two
):
    columns = charges.shape[1]
    leaves = near_list.shape[0]
    nodes = leaves // 8
    tops = nodes // 8
    depth = 4 * (leaves // 64)
    rows, cols = lax.axis_size("row"), lax.axis_size("col")
    merge = cols == 2 and tops == 1
    t1 = transfer_one.reshape(leaves * 32, 32)
    t2 = transfer_two.reshape(nodes * 32, 32)
    shape = jax.ShapeDtypeStruct
    width = 2 * depth * 128
    face = shape((80, width), BF16)
    outs = call(
        functools.partial(face_kernel, merge, depth),
        [shape((64, columns), BF16), shape((16, columns), BF16), face, face] + ([] if merge else [face]),
        [charges, points],
        scratch=[pltpu.VMEM((3, columns), F32), pltpu.SemaphoreType.DMA((2,))],
        hbm_in=2,
    )
    charges, feat, odd = outs[:3]
    up = [(i, i + 1) for i in range(cols - 1)]
    down = [(j, i) for i, j in up]
    if merge:
        left = right = lax.ppermute(outs[3], "col", up + down)
    else:
        left, right = lax.ppermute(outs[3], "col", up), lax.ppermute(outs[4], "col", down)
    odd = lax.ppermute(odd, "row", [p for i in range(1, rows - 1, 2) for p in ((i, i + 1), (i + 1, i))])
    even, coef = call(
        functools.partial(up_kernel, merge, depth),
        [shape((80, width + (128 if merge else 0)), BF16)]
        + [shape((16 * nodes + 32, 128) if merge else ((nodes + tops) * 32, 64), BF16)],
        [charges, feat, leaf_basis, t1, t2],
        flops=1 << 31,
    )
    even = lax.ppermute(even, "row", [(i, i ^ 1) for i in range(rows)])
    sel, sel_x, pick = constants()
    acc_shape = shape((2 * depth, 64, 512), F32)
    acc, x, mask, yt = call(
        functools.partial(own_kernel, depth),
        [
            acc_shape,
            shape((2 * depth, 96, 512), BF16),
            shape((2 * depth, 48, 512), F32),
            shape((2 * depth * SIDE, 128, 32), BF16),
        ],
        [charges, feat, near_list.T, sel, sel_x, pick],
        flops=1 << 32,
    )
    corner = shape((80, depth * 128 + (256 if merge else 0)), BF16)
    packed = call(
        functools.partial(corner_kernel, merge, depth),
        [corner] if merge else [corner, corner],
        [even, odd] + ([coef] if merge else []),
    )
    if merge:
        corner_left = corner_right = lax.ppermute(packed[0], "col", up + down)
        at = depth * 128 + 128
        top = jnp.stack([packed[0][48:80, at:], corner_left[48:80, at:]])
        top = doubled(top, "row", 2)
        one = [coef, corner_left]
    else:
        corner_left = lax.ppermute(packed[0], "col", up)
        corner_right = lax.ppermute(packed[1], "col", down)
        coef = doubled(coef.reshape(1, nodes + tops, 32, 64), "col")
        one = [coef[:, :nodes].reshape(cols * nodes, 32, 64)]
        top = doubled(coef[:, nodes:].reshape(1, cols * tops, 32, 64), "row").reshape(-1, 32, 64)
    acc = call(
        functools.partial(side_kernel, merge, depth),
        acc_shape,
        [charges, right] + ([] if merge else [left]) + [sel, x, mask, yt, acc],
        alias=6 if merge else 7,
        scratch=[pltpu.VMEM((2 * depth * SIDE, 64, 128), BF16), pltpu.VMEM((2 * depth * SIDE, 64, 64), BF16)],
        flops=1 << 32,
    )
    acc, edge_c, edge_y = call(
        functools.partial(edge_kernel, depth),
        [acc_shape, shape((4 * depth, 64, 128), BF16), shape((4 * depth, 128, 32), BF16)],
        [even, odd, sel, x, mask, acc],
        alias=5,
        flops=1 << 31,
    )
    field = call(
        functools.partial(couple_kernel, merge, cols * nodes),
        shape((nodes * 32, 64), F32),
        [couple_one, *one, list_one],
        smem=1,
        scratch=[pltpu.VMEM((2 * nodes + 1, 32, 64), BF16)] if merge else [],
        flops=1 << 30,
    )
    acc = call(
        functools.partial(last_kernel, merge, depth),
        acc_shape,
        [edge_c, edge_y, corner_right] + ([] if merge else [corner_left]) + [sel, x, mask, acc],
        alias=6 if merge else 7,
        scratch=[pltpu.VMEM((4 * depth, 64, 128), BF16), pltpu.VMEM((4 * depth, 64, 64), BF16)],
        flops=1 << 31,
    )
    return call(
        functools.partial(down_kernel, depth, merge),
        shape((64, columns), BF16),
        [acc, field, leaf_basis, t1, t2, couple_two, top, list_two],
        smem=1,
        scratch=[
            pltpu.VMEM((64, columns), BF16),
            pltpu.SemaphoreType.DMA((nodes,)),
            pltpu.VMEM((rows * cols * tops, 32, 64), BF16),
        ],
        hbm_out=True,
    )


def solution(mesh):
    line, block = P(None, ("row", "col")), P(("row", "col"))
    in_specs = (line, line, line) + (block,) * 7

    return jax.shard_map(shards, mesh=mesh, in_specs=in_specs, out_specs=line, check_vma=False)
```

```python
import functools

import jax
import jax.numpy as jnp
import numpy as np
from jax import lax
from jax.experimental import pallas as pl
from jax.experimental.pallas import tpu as pltpu
from jax.sharding import PartitionSpec as P


NEAR = 27
SIDE = 4
SOFTENING = 0.0025
F32 = jnp.float32
BF16 = jnp.bfloat16
NT = (((1,), (1,)), ((), ()))
TN = (((0,), (0,)), ((), ()))
NN = (((1,), (0,)), ((), ()))


def split_layers(depth):
    return range(0, depth // 4), range(depth // 4, depth // 2), range(depth // 2, depth)


VMEM = pl.BlockSpec(memory_space=pltpu.VMEM)
SMEM = pl.BlockSpec(memory_space=pltpu.SMEM)
HBM = pl.BlockSpec(memory_space=pltpu.MemorySpace.HBM)


def dot(a, b, dims=NN):
    return lax.dot_general(a, b, dims, preferred_element_type=F32)


def split2(v):
    hi = v.astype(BF16)
    lo = (v - hi.astype(F32)).astype(BF16)
    return hi, lo


def tile_of(z, y, x1):
    return (z // 4) * 32 + (z // 2 % 2) * 16 + (y // 2) * 8 + x1 * 4 + (z % 2) * 2 + (y % 2)


def lower_half(shape):
    return lax.broadcasted_iota(jnp.int32, shape, len(shape) - 1) % 128 < 64


def swap_matrix():
    a = lax.broadcasted_iota(jnp.int32, (128, 128), 0)
    b = lax.broadcasted_iota(jnp.int32, (128, 128), 1)
    return jnp.where((a + 64) % 128 == b, 1.0, 0.0).astype(BF16)


def block_basis(basis):
    rank, width = basis.shape
    leaf = lax.broadcasted_iota(jnp.int32, (rank, width), 1) // 64
    zero = jnp.zeros_like(basis)
    return jnp.concatenate([jnp.where(leaf == k, basis, zero) for k in range(8)], axis=0)


def feature_rows(x):
    pairs = [split2(v) for v in x]
    hi = [a.astype(F32) for a, _ in pairs]
    lo = [b.astype(F32) for _, b in pairs]
    y = [a + b for a, b in zip(hi, lo)]
    norm = y[0] * y[0] + y[1] * y[1] + y[2] * y[2]
    n1 = norm.astype(BF16).astype(F32)
    n2 = (norm - n1).astype(BF16).astype(F32)
    n3 = norm - n1 - n2
    width = norm.shape[1]
    index = lax.broadcasted_iota(jnp.int32, (16, width), 0)
    out = jnp.where(index == 9, 1.0, 0.0)
    for k, piece in enumerate(hi + lo + [n1, n2, n3]):
        out = jnp.where(index == k, piece, out)
    return out.astype(BF16)


def with_ones(rows):
    index = lax.broadcasted_iota(jnp.int32, rows.shape, 0)
    return jnp.where(index == 9, jnp.ones_like(rows), rows)


def coordinates(rows):
    return [rows[c : c + 1].astype(F32) + rows[c + 3 : c + 4].astype(F32) for c in range(3)]


def swapped(tiles):
    out = dot(jnp.concatenate(tiles, axis=0), swap_matrix()).astype(BF16)
    size = tiles[0].shape[0]
    return [out[size * k : size * k + size] for k in range(len(tiles))]


def halves(firsts, seconds, x1):
    low = lower_half(firsts[0].shape)
    if x1 == 1:
        return [jnp.where(low, a, b) for a, b in zip(swapped(firsts), seconds)]
    return [jnp.where(low, a, b) for a, b in zip(firsts, swapped(seconds))]


def unpacked(rights, lefts):
    low = lower_half(rights[0].shape)
    turned = swapped(rights)
    other = turned if rights is lefts else swapped(lefts)
    return [
        (jnp.where(low, r, o), jnp.where(low, t, l)) for r, l, t, o in zip(rights, lefts, turned, other)
    ]


def tiles_in(ref, first, count):
    return [ref[:, 128 * k : 128 * k + 128] for k in range(first, first + count)]


def transposed(tiles, sel_ref):
    rows = dot(jnp.concatenate(tiles, axis=1), sel_ref[:, 0:32], TN).astype(BF16)
    return [rows[128 * k : 128 * k + 128] for k in range(len(tiles))]


def send_rows(pay_ref, last_first, q_ref, feat, depth):
    width = 2 * depth * 128
    for z in range(depth):
        for k in range(2):
            ats = [tile_of(z, y, k) * 128 for y in (SIDE - 1, 0)]
            at = (z * 2 + k) * 128
            pay_ref[0:64, at : at + 128] = jnp.where(
                last_first, q_ref[:, ats[0] : ats[0] + 128], q_ref[:, ats[1] : ats[1] + 128]
            )
            pay_ref[64:80, at : at + 128] = jnp.where(
                last_first, feat[:, ats[0] : ats[0] + 128], feat[:, ats[1] : ats[1] + 128]
            )
    x = coordinates(pay_ref[64:80, 0:width].astype(F32))
    shift = jnp.where(last_first, -float(SIDE), float(SIDE))
    pay_ref[64:80, 0:width] = feature_rows([x[0], x[1] + shift, x[2]])


def face_kernel(merge, depth, q_ref, pts_ref, *refs):
    if merge:
        coef_ref, *refs = refs
    feat_ref, even_ref, odd_ref, xpay_ref, *more = refs
    row, col = lax.axis_index("row"), lax.axis_index("col")
    columns = q_ref.shape[1]
    centre = (
        (SIDE * col + SIDE // 2).astype(F32),
        (SIDE * row + SIDE // 2).astype(F32),
        jnp.float32(depth / 2),
    )
    local = [pts_ref[c : c + 1, :] - centre[c] for c in range(3)]
    feat = feature_rows(local)
    feat_ref[...] = feat
    pair_x = lax.broadcasted_iota(jnp.int32, (1, columns), 1) // 512 % 2
    shift = jnp.where(pair_x == 1, -float(SIDE), float(SIDE))
    moved = feature_rows([local[0] + shift, local[1], local[2]])

    def tile(z, y, x1):
        at = tile_of(z, y, x1) * 128
        return jnp.concatenate([q_ref[:, at : at + 128], moved[:, at : at + 128]], axis=0)

    places = [(z, y1) for z in range(depth) for y1 in range(2)]
    sides = [[[tile(z, 2 * y1 + k, x1) for z, y1 in places] for k in range(2)] for x1 in range(2)]
    if merge:
        first = [jnp.where(col == 0, a, b) for a, b in zip(sides[1][0], sides[0][1])]
        second = [jnp.where(col == 0, a, b) for a, b in zip(sides[1][1], sides[0][0])]
        low = lower_half((80, 128)) == (col == 0)
        for k, (a, b) in enumerate(zip(swapped(first), second)):
            xpay_ref[:, 128 * k : 128 * k + 128] = jnp.where(low, a, b)
        width = 2 * depth * 128
        blocks = jnp.concatenate([coef_ref[...], jnp.zeros((160 - coef_ref.shape[0], 128), BF16)], axis=0)
        for k in range(2):
            xpay_ref[:, width + 128 * k : width + 128 * k + 128] = blocks[80 * k : 80 * k + 80]
    else:
        for ref, x1 in ((xpay_ref, 1), (more[0], 0)):
            for k, value in enumerate(halves(*sides[x1], x1)):
                ref[:, 128 * k : 128 * k + 128] = value
    send_rows(odd_ref, row % 2 == 1, q_ref, feat, depth)
    send_rows(even_ref, row % 2 == 0, q_ref, feat, depth)


def up_kernel(merge, q_ref, basis_ref, t1_ref, t2_ref, *refs):
    if merge:
        coef_ref, top_ref = refs
    else:
        coef_ref = refs[0]
    nodes = q_ref.shape[1] // 512
    leaf = []
    for n in range(nodes):
        chunk = slice(512 * n, 512 * n + 512)
        leaf.append(dot(block_basis(basis_ref[:, chunk]), q_ref[:, chunk], NT).astype(BF16))
    ones = [dot(t1_ref[256 * n : 256 * n + 256, :], leaf[n], TN).astype(BF16) for n in range(nodes)]
    tops = []
    for m in range(nodes // 8):
        part = jnp.concatenate(ones[8 * m : 8 * m + 8], axis=0)
        tops.append(dot(t2_ref[256 * m : 256 * m + 256, :], part, TN).astype(BF16))
    if merge:
        pairs = [jnp.concatenate([ones[2 * k], ones[2 * k + 1]], axis=1) for k in range(nodes // 2)]
        for k, value in enumerate(pairs):
            coef_ref[32 * k : 32 * k + 32, :] = value
        top_ref[0] = tops[0]
    else:
        for k, value in enumerate(ones + tops):
            coef_ref[32 * k : 32 * k + 32, :] = value


def row_sides(even_ref, odd_ref):
    even = lax.axis_index("row") % 2 == 0

    def face(side, at):
        a, b = even_ref[:, at : at + 128], odd_ref[:, at : at + 128]
        return jnp.where(even, b, a) if side == 0 else jnp.where(even, a, b)

    return face


def corner_kernel(merge, depth, even_ref, odd_ref, *refs):
    col = lax.axis_index("col")
    face = row_sides(even_ref, odd_ref)
    pay_ref = refs[0]
    tiles = [[[face(side, (z * 2 + k) * 128) for z in range(depth)] for side in range(2)] for k in range(2)]
    high, base = halves(*tiles[1], 1), halves(*tiles[0], 0)
    groups = [(pay_ref, jnp.concatenate(high, axis=1), -float(SIDE))]
    if merge:
        mine = jnp.where(col == 0, groups[0][1], jnp.concatenate(base, axis=1))
        groups = [(pay_ref, mine, jnp.where(col == 0, -float(SIDE), float(SIDE)))]
    else:
        groups.append((refs[1], jnp.concatenate(base, axis=1), float(SIDE)))
    width = depth * 128
    for ref, tile, shift in groups:
        ref[0:64, 0:width] = tile[0:64]
        x = coordinates(tile[64:80].astype(F32))
        ref[64:80, 0:width] = feature_rows([x[0] + shift, x[1], x[2]])


def tops_kernel(top_ref, out_ref):
    half = out_ref.shape[0]
    for k in range(half):
        out_ref[k] = jnp.concatenate([top_ref[k], top_ref[half + k]], axis=1)


def layers_of(depth, tz):
    return [sz for sz in (tz - 1, tz, tz + 1) if 0 <= sz < depth]


def inner_steps(depth, targets):
    steps = []
    for tz in targets:
        layers = layers_of(depth, tz)
        for sz in layers:
            steps.append((tz, (0, 1), [(sz, 1), (sz, 2)]))
            steps.append((tz, (2, 3), [(sz, 3), (sz, 4)]))
        steps.append((tz, (1,), [(sz, 3) for sz in layers]))
        steps.append((tz, (2,), [(sz, 2) for sz in layers]))
    return steps


def mask_row(mask_ref, at, dz, dy, k, ty):
    row = dz * 16 + dy * 4 + k
    m = mask_ref[at, row : row + 1, 128 * ty : 128 * ty + 128]
    m = jnp.broadcast_to(m, (16, 128)).astype(BF16)
    return jnp.concatenate([m] * 4, axis=0)


AHEAD = 6


def scan(steps, depth, rows_of, charge_of, x_ref, mask_ref, acc_ref, fresh=False):
    steps = [(xp, *step) for xp in range(2) for step in steps]

    def pair():
        ready, seen = [], set()
        for i in range(len(steps) + AHEAD):
            if i < len(steps):
                xp, sides, (tz, tiles, sources) = steps[i]
                lanes = slice(128 * tiles[0], 128 * tiles[-1] + 128)
                at = xp * depth + tz
                rows = jnp.concatenate([rows_of(sides, xp, sz, ye) for sz, ye in sources], axis=0)
                features = x_ref[at, 32:96, lanes] if sides else x_ref[at, 0:32, lanes]
                ready.append(lax.rsqrt(dot(rows, features).astype(BF16)))
            if i >= AHEAD:
                xp, sides, (tz, tiles, sources) = steps[i - AHEAD]
                inv, ready[i - AHEAD] = ready[i - AHEAD], None
                lanes = slice(128 * tiles[0], 128 * tiles[-1] + 128)
                at = xp * depth + tz
                size = 64 if sides else 128
                columns = []
                for j, ty in enumerate(tiles):
                    blocks = []
                    for k, (sz, ye) in enumerate(sources):
                        part = inv[size * k : size * k + size, 128 * j : 128 * j + 128]
                        halves = [part, part] if sides else [part[0:64], part[64:128]]
                        first = 2 if sides else 0
                        blocks += [
                            h * mask_row(mask_ref, at, sz - tz + 1, ye - ty, first + c, ty) for c, h in enumerate(halves)
                        ]
                    columns.append(jnp.concatenate(blocks, axis=0))
                kernel = columns[0] if len(columns) == 1 else jnp.concatenate(columns, axis=1)
                charge = jnp.concatenate([charge_of(sides, xp, sz, ye) for sz, ye in sources], axis=1)
                value = dot(charge, kernel)
                if fresh and len(tiles) == 2 and (xp, tz, tiles) not in seen:
                    seen.add((xp, tz, tiles))
                    acc_ref[at, :, lanes] = value
                else:
                    acc_ref[at, :, lanes] += value

    pair()


def own_kernel(depth, targets, q_ref, feat_ref, nl_ref, sel_ref, sel_x_ref, pick_ref, acc_ref, x_ref, mask_ref, yt_ref):
    columns = q_ref.shape[1]
    leaves = columns // 64
    x = dot(sel_x_ref[...], feat_ref[...])
    active = jnp.where(nl_ref[...] >= 0, 1.0, 0.0).astype(BF16)
    pick = dot(pick_ref[...], active)
    pick = jnp.where(
        lax.broadcasted_iota(jnp.int32, (48, leaves), 1) % 2 == 0, pick[0:48], pick[48:96]
    ).astype(BF16)
    spread = jnp.where(
        lax.broadcasted_iota(jnp.int32, (leaves, columns), 0)
        == lax.broadcasted_iota(jnp.int32, (leaves, columns), 1) // 64,
        1.0,
        0.0,
    ).astype(BF16)
    masks = dot(pick, spread)
    low = lower_half((32, 128))
    rows = dot(feat_ref[...], sel_ref[:, 0:32], TN).astype(BF16)
    for z in range(depth):
        for xp in range(2):
            for y in range(SIDE):
                at = tile_of(z, y, xp) * 128
                lanes = slice(128 * y, 128 * y + 128)
                tile = x[:, at : at + 128]
                x_ref[xp * depth + z, 0:32, lanes] = tile.astype(BF16)
                x_ref[xp * depth + z, 32:64, lanes] = jnp.where(low, 0.0, tile).astype(BF16)
                x_ref[xp * depth + z, 64:96, lanes] = jnp.where(low, tile, 0.0).astype(BF16)
                mask_ref[xp * depth + z, :, lanes] = masks[:, at : at + 128]
                yt_ref[(xp * depth + z) * SIDE + y] = rows[at : at + 128]

    own_steps(depth, targets, q_ref, x_ref, mask_ref, yt_ref, acc_ref)


def own_steps(depth, targets, q_ref, x_ref, mask_ref, yt_ref, acc_ref):
    def rows_of(sides, xp, sz, ye):
        return yt_ref[(xp * depth + sz) * SIDE + ye - 1]

    def charge_of(sides, xp, sz, ye):
        base = tile_of(sz, ye - 1, xp) * 128
        return q_ref[:, base : base + 128]

    steps = [(False, step) for step in inner_steps(depth, targets)]
    scan(steps, depth, rows_of, charge_of, x_ref, mask_ref, acc_ref, fresh=True)


def more_own_kernel(depth, targets, q_ref, x_ref, mask_ref, yt_ref, in_ref, acc_ref):
    own_steps(depth, targets, q_ref, x_ref, mask_ref, yt_ref, acc_ref)


def beside(right, left):
    return jnp.concatenate([right, left], axis=1)


def side_kernel(merge, depth, targets, q_ref, right_ref, *refs):
    if not merge:
        left_ref, *refs = refs
    sel_ref, x_ref, mask_ref, yt_ref, _, acc_ref, c_ref, ys_ref = refs
    low = lower_half((64, 128))
    count = 2 * depth
    rights = tiles_in(right_ref, 0, count)
    lefts = rights if merge else tiles_in(left_ref, 0, count)
    beyond = [tile for pair in unpacked(rights, lefts) for tile in pair]
    turned = transposed([with_ones(h[64:80]) for h in beyond], sel_ref)
    for z in range(depth):
        for y in range(SIDE):
            t = [q_ref[:, a * 128 : a * 128 + 128] for a in (tile_of(z, y, 0), tile_of(z, y, 1))]
            even, odd = z * SIDE + y, (depth + z) * SIDE + y
            h, rows = beyond[even][0:64], turned[even]
            c_ref[even] = jnp.where(low, t[1], h)
            c_ref[odd] = jnp.where(low, h, t[0])
            ys_ref[even] = beside(yt_ref[odd, 0:64], rows[64:128])
            ys_ref[odd] = beside(rows[0:64], yt_ref[even, 64:128])

    side_steps(depth, targets, x_ref, mask_ref, c_ref, ys_ref, acc_ref)


def side_steps(depth, targets, x_ref, mask_ref, c_ref, ys_ref, acc_ref):
    def rows_of(sides, xp, sz, ye):
        return ys_ref[(xp * depth + sz) * SIDE + ye - 1]

    def charge_of(sides, xp, sz, ye):
        return c_ref[(xp * depth + sz) * SIDE + ye - 1]

    steps = [(True, step) for step in inner_steps(depth, targets)]
    scan(steps, depth, rows_of, charge_of, x_ref, mask_ref, acc_ref)


def more_side_kernel(depth, targets, x_ref, mask_ref, c_ref, ys_ref, in_ref, acc_ref):
    side_steps(depth, targets, x_ref, mask_ref, c_ref, ys_ref, acc_ref)


def edge_steps(depth, sides):
    steps = []
    for tz in range(depth):
        for side in range(2):
            sources = [(sz, side * (SIDE + 1)) for sz in layers_of(depth, tz)]
            steps.append((sides, (tz, (side * (SIDE - 1),), sources)))
    return steps


def edge_kernel(depth, even_ref, odd_ref, sel_ref, x_ref, mask_ref, in_ref, acc_ref, c_ref, yt_ref):
    face = row_sides(even_ref, odd_ref)
    places = [(k, z, side) for k in range(2) for z in range(depth) for side in range(2)]
    tiles = [face(side, (z * 2 + k) * 128) for k, z, side in places]
    for i, rows in enumerate(transposed([with_ones(tile[64:80]) for tile in tiles], sel_ref)):
        c_ref[i] = tiles[i][0:64]
        yt_ref[i] = rows

    def rows_of(sides, xp, sz, ye):
        return yt_ref[(xp * depth + sz) * 2 + (ye > 0)]

    def charge_of(sides, xp, sz, ye):
        return c_ref[(xp * depth + sz) * 2 + (ye > 0)]

    scan(edge_steps(depth, False), depth, rows_of, charge_of, x_ref, mask_ref, acc_ref)


def last_kernel(merge, depth, edge_c_ref, edge_y_ref, right_ref, *refs):
    if not merge:
        left_ref, *refs = refs
    sel_ref, x_ref, mask_ref, _, acc_ref, c_ref, ys_ref = refs
    low = lower_half((64, 128))
    rights = tiles_in(right_ref, 0, depth)
    lefts = rights if merge else tiles_in(left_ref, 0, depth)
    beyond = [tile for pair in unpacked(rights, lefts) for tile in pair]
    turned = transposed([with_ones(h[64:80]) for h in beyond], sel_ref)
    for z in range(depth):
        for side in range(2):
            even, odd = z * 2 + side, (depth + z) * 2 + side
            h, rows = beyond[even][0:64], turned[even]
            c_ref[even] = jnp.where(low, edge_c_ref[odd], h)
            c_ref[odd] = jnp.where(low, h, edge_c_ref[even])
            ys_ref[even] = beside(edge_y_ref[odd, 0:64], rows[64:128])
            ys_ref[odd] = beside(rows[0:64], edge_y_ref[even, 64:128])

    def rows_of(sides, xp, sz, ye):
        return ys_ref[(xp * depth + sz) * 2 + (ye > 0)]

    def charge_of(sides, xp, sz, ye):
        return c_ref[(xp * depth + sz) * 2 + (ye > 0)]

    scan(edge_steps(depth, True), depth, rows_of, charge_of, x_ref, mask_ref, acc_ref)


def couple_kernel(merge, group, k1_ref, *refs):
    col = lax.axis_index("col")
    if merge:
        own_ref, got_ref, l1_ref, out_ref, coef_ref = refs
        nodes = l1_ref.shape[0]
        at = got_ref.shape[1] - 256
        got = jnp.concatenate([got_ref[:, at : at + 128], got_ref[:, at + 128 : at + 256]], axis=0)
        for k in range(nodes // 2):
            for side, value in enumerate((own_ref[32 * k : 32 * k + 32, :], got[32 * k : 32 * k + 32])):
                coef_ref[side * nodes + 2 * k] = value[:, 0:64]
                coef_ref[side * nodes + 2 * k + 1] = value[:, 64:128]
        coef_ref[group] = jnp.zeros((32, 64), BF16)
    else:
        coef_ref, l1_ref, out_ref = refs
    nodes, slots = l1_ref.shape
    mask = col * nodes
    zero = jnp.zeros((32, 64), BF16)
    totals = []
    for n in range(nodes):
        parts = []
        for s in range(slots):
            v = l1_ref[n, s]
            at = (v & (group - 1)) ^ mask
            if merge:
                parts.append(coef_ref[jnp.where(v >= 0, at, group)])
            else:
                parts.append(jnp.where(v >= 0, coef_ref[at], zero))
        matrix = jnp.concatenate([k1_ref[n, s] for s in range(slots)], axis=1)
        totals.append(dot(matrix, jnp.concatenate(parts, axis=0)))
    for n in range(nodes):
        out_ref[32 * n : 32 * n + 32, :] = totals[n]


def down_kernel(depth, merge, acc_ref, f1_ref, basis_ref, t1_ref, t2_ref, k2_ref, top_ref, *refs):
    if merge:
        got_ref, *refs = refs
    l2_ref, out_hbm, out_ref, sems, top_scr = refs
    row, col = lax.axis_index("row"), lax.axis_index("col")
    nodes = out_hbm.shape[1] // 512
    per = nodes // 8
    me = row * lax.axis_size("col") + col
    if merge:
        count = top_ref.shape[0]
        bits = count.bit_length() - 1
        place = [sum(((k >> b) & 1) << (bits - 1 - b) for b in range(bits)) for k in range(count)]
        for k in range(count // 2):
            block = got_ref[k]
            top_scr[2 * place[k] + 1] = block[:, 0:64]
            top_scr[2 * place[k + count // 2] + 1] = block[:, 64:128]
        for k in range(count):
            top_scr[2 * place[k]] = top_ref[k]
    else:
        top_scr[...] = top_ref[...]
    copies = []
    for m in range(per):
        parts = []
        for s in range(l2_ref.shape[1]):
            v = l2_ref[m, s]
            at = v ^ me if per == 1 else ((v // per) ^ me) * per + v % per
            parts.append(top_scr[at])
        matrix = jnp.concatenate([k2_ref[m, s] for s in range(l2_ref.shape[1])], axis=1)
        hi2, lo2 = split2(dot(matrix, jnp.concatenate(parts, axis=0)))
        t2 = t2_ref[256 * m : 256 * m + 256, :]
        hi1, lo1 = split2(f1_ref[256 * m : 256 * m + 256, :] + dot(t2, hi2) + dot(t2, lo2))
        leaves = []
        for j in range(8):
            n = 8 * m + j
            t1 = t1_ref[256 * n : 256 * n + 256, :]
            rows = slice(32 * j, 32 * j + 32)
            leaves.append((dot(t1, hi1[rows]) + dot(t1, lo1[rows])).astype(BF16))
        for j in range(8):
            n = 8 * m + j
            far = dot(leaves[j], block_basis(basis_ref[:, 512 * n : 512 * n + 512]), TN)
            z1, y1, x1 = j // 4, j // 2 % 2, j % 2
            for k in range(4):
                z, y = 4 * m + 2 * z1 + k // 2, 2 * y1 + k % 2
                part = acc_ref[x1 * depth + z, :, 128 * y : 128 * y + 128]
                total = part * (NEAR * 64) ** (-0.5) + far[:, 128 * k : 128 * k + 128]
                out_ref[:, 512 * n + 128 * k : 512 * n + 128 * k + 128] = total.astype(BF16)
            lanes = pl.ds(512 * n, 512)
            copies.append(pltpu.make_async_copy(out_ref.at[:, lanes], out_hbm.at[:, lanes], sems.at[n]))
            copies[-1].start()
    for copy in copies:
        copy.wait()


def constants():
    sel = np.zeros((16, 160), np.float32)
    sel_x = np.zeros((32, 16), np.float32)
    rest, eps = np.float32(SOFTENING), []
    for _ in range(3):
        eps.append(np.asarray(rest).astype(jnp.bfloat16).astype(np.float32))
        rest = np.float32(rest - eps[-1])
    for f in range(21):
        source = f if f < 6 else f - 6 if f < 12 else 9 if f < 15 else f - 9 if f < 18 else 9
        for base in (0, 32, 128):
            sel[source, base + f] = 1
        if f < 12:
            sel_x[f, f % 3 + (3 if f >= 6 else 0)] = -2
        elif f < 15:
            sel_x[f, f - 6] = 1
        else:
            sel_x[f, 9] = 1 if f < 18 else eps[f - 18]
    pick = np.zeros((96, NEAR), np.float32)
    for dz in range(3):
        for dy in range(3):
            for k in range(4):
                for half, dx in enumerate(((0, 1, None, -1)[k], (-1, 0, 1, None)[k])):
                    if dx is not None:
                        pick[48 * half + dz * 16 + dy * 4 + k, 9 * dz + 3 * dy + dx + 1] = 1
    return [jnp.asarray(v, BF16) for v in (sel, sel_x, pick)]


def permuted(value, axis, pairs):
    return lax.ppermute(value, axis, pairs)


def doubled(value, axis, start=1):
    size = lax.axis_size(axis)
    step = start
    while step < size:
        other = permuted(value, axis, [(i, i ^ step) for i in range(size)])
        value = jnp.concatenate([value, other], axis=0)
        step *= 2
    return value


def call(kernel, out_shape, ins, smem=0, scratch=(), flops=0, alias=None, hbm_in=0, hbm_out=False):
    single = not isinstance(out_shape, list)
    return pallas(kernel, out_shape, ins, smem, scratch, flops, alias, single, hbm_in, hbm_out)


def pallas(kernel, out_shape, ins, smem, scratch, flops, alias, single, hbm_in, hbm_out):
    return pl.pallas_call(
        kernel,
        out_shape=out_shape,
        in_specs=[HBM] * hbm_in + [VMEM] * (len(ins) - smem - hbm_in) + [SMEM] * smem,
        out_specs=(HBM if hbm_out else VMEM) if single else [VMEM] * len(out_shape),
        scratch_shapes=list(scratch),
        input_output_aliases={alias: 0} if alias is not None else {},
        compiler_params=pltpu.CompilerParams(vmem_limit_bytes=40 * 1024 * 1024),
        cost_estimate=pl.CostEstimate(flops=flops, bytes_accessed=1 << 20, transcendentals=0) if flops else None,
    )(*ins)


def shards(
    charges, points, leaf_basis, transfer_one, transfer_two, couple_one, couple_two, near_list, list_one, list_two
):
    columns = charges.shape[1]
    leaves = near_list.shape[0]
    nodes = leaves // 8
    tops = nodes // 8
    depth = 4 * (leaves // 64)
    rows, cols = lax.axis_size("row"), lax.axis_size("col")
    merge = cols == 2 and tops == 1
    t1 = transfer_one.reshape(leaves * 32, 32)
    t2 = transfer_two.reshape(nodes * 32, 32)
    shape = jax.ShapeDtypeStruct
    width = 2 * depth * 128
    face = shape((80, width), BF16)
    up = [(i, i + 1) for i in range(cols - 1)]
    down = [(j, i) for i, j in up]
    corner_width = depth * 128
    ups = call(
        functools.partial(up_kernel, merge),
        [shape((16 * nodes, 128), BF16), shape((1, 32, 64), BF16)]
        if merge
        else [shape(((nodes + tops) * 32, 64), BF16)],
        [charges, leaf_basis, t1, t2],
        flops=1 << 31,
    )
    coef = ups[0]
    outs = call(
        functools.partial(face_kernel, merge, depth),
        [shape((16, columns), BF16), face, face]
        + ([shape((80, width + 256), BF16)] if merge else [face, face]),
        [charges, points] + ([coef] if merge else []),
        flops=1 << 31,
    )
    feat, even, odd, pay = outs[:4]
    odd = permuted(odd, "row", [p for i in range(1, rows - 1, 2) for p in ((i, i + 1), (i + 1, i))])
    even = permuted(even, "row", [(i, i ^ 1) for i in range(rows)])
    if merge:
        left = right = permuted(pay, "col", up + down)
        top = ups[1]
        step = rows // 2
        while step:
            other = permuted(top, "row", [(i, i ^ step) for i in range(rows)])
            top = jnp.concatenate([top, other], axis=0)
            step //= 2
        one = [coef, right]
    else:
        left, right = permuted(pay, "col", up), permuted(outs[4], "col", down)
        coef = doubled(coef.reshape(1, nodes + tops, 32, 64), "col")
        one = [coef[:, :nodes].reshape(cols * nodes, 32, 64)]
        top = doubled(coef[:, nodes:].reshape(1, cols * tops, 32, 64), "row").reshape(-1, 32, 64)
    sel, sel_x, pick = constants()
    acc_shape = shape((2 * depth, 64, 512), F32)
    first, second, third = split_layers(depth)
    acc, x, mask, yt = call(
        functools.partial(own_kernel, depth, first),
        [
            acc_shape,
            shape((2 * depth, 96, 512), BF16),
            shape((2 * depth, 48, 512), F32),
            shape((2 * depth * SIDE, 128, 32), BF16),
        ],
        [charges, feat, near_list.T, sel, sel_x, pick],
        flops=1 << 32,
    )
    for targets in (second, third):
        acc = call(
            functools.partial(more_own_kernel, depth, targets),
            acc_shape,
            [charges, x, mask, yt, acc],
            alias=4,
            flops=1 << 31,
        )
    corner = shape((80, corner_width), BF16)
    packed = call(functools.partial(corner_kernel, merge, depth), [corner] if merge else [corner, corner], [even, odd])
    if merge:
        corner_left = corner_right = permuted(packed[0], "col", up + down)
        got = call(tops_kernel, shape((rows // 2, 32, 128), BF16), [top])
        got = permuted(got, "col", up + down)
    else:
        corner_left = permuted(packed[0], "col", up)
        corner_right = permuted(packed[1], "col", down)
    acc, side_c, side_y = call(
        functools.partial(side_kernel, merge, depth, range(0, depth // 2)),
        [acc_shape, shape((2 * depth * SIDE, 64, 128), BF16), shape((2 * depth * SIDE, 64, 64), BF16)],
        [charges, right] + ([] if merge else [left]) + [sel, x, mask, yt, acc],
        alias=6 if merge else 7,
        flops=1 << 32,
    )
    acc = call(
        functools.partial(more_side_kernel, depth, range(depth // 2, depth)),
        acc_shape,
        [x, mask, side_c, side_y, acc],
        alias=4,
        flops=1 << 31,
    )
    acc, edge_c, edge_y = call(
        functools.partial(edge_kernel, depth),
        [acc_shape, shape((4 * depth, 64, 128), BF16), shape((4 * depth, 128, 32), BF16)],
        [even, odd, sel, x, mask, acc],
        alias=5,
        flops=1 << 31,
    )
    field = call(
        functools.partial(couple_kernel, merge, cols * nodes),
        shape((nodes * 32, 64), F32),
        [couple_one, *one, list_one],
        smem=1,
        scratch=[pltpu.VMEM((2 * nodes + 1, 32, 64), BF16)] if merge else [],
        flops=1 << 30,
    )
    acc = call(
        functools.partial(last_kernel, merge, depth),
        acc_shape,
        [edge_c, edge_y, corner_right] + ([] if merge else [corner_left]) + [sel, x, mask, acc],
        alias=6 if merge else 7,
        scratch=[pltpu.VMEM((4 * depth, 64, 128), BF16), pltpu.VMEM((4 * depth, 64, 64), BF16)],
        flops=1 << 31,
    )
    return call(
        functools.partial(down_kernel, depth, merge),
        shape((64, columns), BF16),
        [acc, field, leaf_basis, t1, t2, couple_two, top] + ([got] if merge else []) + [list_two],
        smem=1,
        scratch=[
            pltpu.VMEM((64, columns), BF16),
            pltpu.SemaphoreType.DMA((nodes,)),
            pltpu.VMEM((rows * cols * tops, 32, 64), BF16),
        ],
        hbm_out=True,
    )


def solution(mesh):
    line, block = P(None, ("row", "col")), P(("row", "col"))
    in_specs = (line, line, line) + (block,) * 7

    return jax.shard_map(shards, mesh=mesh, in_specs=in_specs, out_specs=line, check_vma=False)
```

```python
import functools

import jax
import jax.numpy as jnp
import numpy as np
from jax import lax
from jax.experimental import pallas as pl
from jax.experimental.pallas import tpu as pltpu
from jax.sharding import PartitionSpec as P


NEAR = 27
SIDE = 4
SOFTENING = 0.0025
F32 = jnp.float32
BF16 = jnp.bfloat16
NT = (((1,), (1,)), ((), ()))
TN = (((0,), (0,)), ((), ()))
NN = (((1,), (0,)), ((), ()))


def split_layers(depth):
    return range(0, depth // 4), range(depth // 4, depth // 2), range(depth // 2, depth)


VMEM = pl.BlockSpec(memory_space=pltpu.VMEM)
SMEM = pl.BlockSpec(memory_space=pltpu.SMEM)
HBM = pl.BlockSpec(memory_space=pltpu.MemorySpace.HBM)


def dot(a, b, dims=NN):
    return lax.dot_general(a, b, dims, preferred_element_type=F32)


def split2(v):
    hi = v.astype(BF16)
    lo = (v - hi.astype(F32)).astype(BF16)
    return hi, lo


def tile_of(z, y, x1):
    return (z // 4) * 32 + (z // 2 % 2) * 16 + (y // 2) * 8 + x1 * 4 + (z % 2) * 2 + (y % 2)


def lower_half(shape):
    return lax.broadcasted_iota(jnp.int32, shape, len(shape) - 1) % 128 < 64


def swap_matrix():
    a = lax.broadcasted_iota(jnp.int32, (128, 128), 0)
    b = lax.broadcasted_iota(jnp.int32, (128, 128), 1)
    return jnp.where((a + 64) % 128 == b, 1.0, 0.0).astype(BF16)


def block_basis(basis):
    rank, width = basis.shape
    leaf = lax.broadcasted_iota(jnp.int32, (rank, width), 1) // 64
    zero = jnp.zeros_like(basis)
    return jnp.concatenate([jnp.where(leaf == k, basis, zero) for k in range(8)], axis=0)


def feature_rows(x):
    pairs = [split2(v) for v in x]
    hi = [a.astype(F32) for a, _ in pairs]
    lo = [b.astype(F32) for _, b in pairs]
    y = [a + b for a, b in zip(hi, lo)]
    norm = y[0] * y[0] + y[1] * y[1] + y[2] * y[2]
    n1 = norm.astype(BF16).astype(F32)
    n2 = (norm - n1).astype(BF16).astype(F32)
    n3 = norm - n1 - n2
    width = norm.shape[1]
    index = lax.broadcasted_iota(jnp.int32, (16, width), 0)
    out = jnp.where(index == 9, 1.0, 0.0)
    for k, piece in enumerate(hi + lo + [n1, n2, n3]):
        out = jnp.where(index == k, piece, out)
    return out.astype(BF16)


def with_ones(rows):
    index = lax.broadcasted_iota(jnp.int32, rows.shape, 0)
    return jnp.where(index == 9, jnp.ones_like(rows), rows)


def coordinates(rows):
    return [rows[c : c + 1].astype(F32) + rows[c + 3 : c + 4].astype(F32) for c in range(3)]


def swapped(tiles):
    out = dot(jnp.concatenate(tiles, axis=0), swap_matrix()).astype(BF16)
    size = tiles[0].shape[0]
    return [out[size * k : size * k + size] for k in range(len(tiles))]


def halves(firsts, seconds, x1):
    low = lower_half(firsts[0].shape)
    if x1 == 1:
        return [jnp.where(low, a, b) for a, b in zip(swapped(firsts), seconds)]
    return [jnp.where(low, a, b) for a, b in zip(firsts, swapped(seconds))]


def unpacked(rights, lefts):
    low = lower_half(rights[0].shape)
    turned = swapped(rights)
    other = turned if rights is lefts else swapped(lefts)
    return [
        (jnp.where(low, r, o), jnp.where(low, t, l)) for r, l, t, o in zip(rights, lefts, turned, other)
    ]


def tiles_in(ref, first, count):
    return [ref[:, 128 * k : 128 * k + 128] for k in range(first, first + count)]


def transposed(tiles, sel_ref):
    rows = dot(jnp.concatenate(tiles, axis=1), sel_ref[:, 0:32], TN).astype(BF16)
    return [rows[128 * k : 128 * k + 128] for k in range(len(tiles))]


def send_rows(pay_ref, last_first, q_ref, feat, depth):
    width = 2 * depth * 128
    for z in range(depth):
        for k in range(2):
            ats = [tile_of(z, y, k) * 128 for y in (SIDE - 1, 0)]
            at = (z * 2 + k) * 128
            pay_ref[0:64, at : at + 128] = jnp.where(
                last_first, q_ref[:, ats[0] : ats[0] + 128], q_ref[:, ats[1] : ats[1] + 128]
            )
            pay_ref[64:80, at : at + 128] = jnp.where(
                last_first, feat[:, ats[0] : ats[0] + 128], feat[:, ats[1] : ats[1] + 128]
            )
    x = coordinates(pay_ref[64:80, 0:width].astype(F32))
    shift = jnp.where(last_first, -float(SIDE), float(SIDE))
    pay_ref[64:80, 0:width] = feature_rows([x[0], x[1] + shift, x[2]])


def face_kernel(merge, depth, q_ref, pts_ref, *refs):
    if merge:
        coef_ref, *refs = refs
    feat_ref, even_ref, odd_ref, xpay_ref, *more = refs
    row, col = lax.axis_index("row"), lax.axis_index("col")
    columns = q_ref.shape[1]
    centre = (
        (SIDE * col + SIDE // 2).astype(F32),
        (SIDE * row + SIDE // 2).astype(F32),
        jnp.float32(depth / 2),
    )
    local = [pts_ref[c : c + 1, :] - centre[c] for c in range(3)]
    feat = feature_rows(local)
    feat_ref[...] = feat
    pair_x = lax.broadcasted_iota(jnp.int32, (1, columns), 1) // 512 % 2
    shift = jnp.where(pair_x == 1, -float(SIDE), float(SIDE))
    moved = feature_rows([local[0] + shift, local[1], local[2]])

    def tile(z, y, x1):
        at = tile_of(z, y, x1) * 128
        return jnp.concatenate([q_ref[:, at : at + 128], moved[:, at : at + 128]], axis=0)

    places = [(z, y1) for z in range(depth) for y1 in range(2)]
    sides = [[[tile(z, 2 * y1 + k, x1) for z, y1 in places] for k in range(2)] for x1 in range(2)]
    if merge:
        first = [jnp.where(col == 0, a, b) for a, b in zip(sides[1][0], sides[0][1])]
        second = [jnp.where(col == 0, a, b) for a, b in zip(sides[1][1], sides[0][0])]
        low = lower_half((80, 128)) == (col == 0)
        for k, (a, b) in enumerate(zip(swapped(first), second)):
            xpay_ref[:, 128 * k : 128 * k + 128] = jnp.where(low, a, b)
        width = 2 * depth * 128
        blocks = jnp.concatenate([coef_ref[...], jnp.zeros((160 - coef_ref.shape[0], 128), BF16)], axis=0)
        for k in range(2):
            xpay_ref[:, width + 128 * k : width + 128 * k + 128] = blocks[80 * k : 80 * k + 80]
    else:
        for ref, x1 in ((xpay_ref, 1), (more[0], 0)):
            for k, value in enumerate(halves(*sides[x1], x1)):
                ref[:, 128 * k : 128 * k + 128] = value
    send_rows(odd_ref, row % 2 == 1, q_ref, feat, depth)
    send_rows(even_ref, row % 2 == 0, q_ref, feat, depth)


def leaf_kernel(q_ref, basis_ref, out_ref):
    for n in range(out_ref.shape[0]):
        chunk = slice(512 * n, 512 * n + 512)
        out_ref[n] = dot(block_basis(basis_ref[:, chunk]), q_ref[:, chunk], NT).astype(BF16)


def up_kernel(merge, leaf_ref, t1_ref, t2_ref, *refs):
    if merge:
        coef_ref, top_ref = refs
    else:
        coef_ref = refs[0]
    nodes = leaf_ref.shape[0]
    ones = [dot(t1_ref[256 * n : 256 * n + 256, :], leaf_ref[n], TN).astype(BF16) for n in range(nodes)]
    tops = []
    for m in range(nodes // 8):
        part = jnp.concatenate(ones[8 * m : 8 * m + 8], axis=0)
        tops.append(dot(t2_ref[256 * m : 256 * m + 256, :], part, TN).astype(BF16))
    if merge:
        pairs = [jnp.concatenate([ones[2 * k], ones[2 * k + 1]], axis=1) for k in range(nodes // 2)]
        for k, value in enumerate(pairs):
            coef_ref[32 * k : 32 * k + 32, :] = value
        top_ref[0] = tops[0]
    else:
        for k, value in enumerate(ones + tops):
            coef_ref[32 * k : 32 * k + 32, :] = value


def row_sides(even_ref, odd_ref):
    even = lax.axis_index("row") % 2 == 0

    def face(side, at):
        a, b = even_ref[:, at : at + 128], odd_ref[:, at : at + 128]
        return jnp.where(even, b, a) if side == 0 else jnp.where(even, a, b)

    return face


def corner_kernel(merge, depth, even_ref, odd_ref, *refs):
    col = lax.axis_index("col")
    face = row_sides(even_ref, odd_ref)
    pay_ref = refs[0]
    tiles = [[[face(side, (z * 2 + k) * 128) for z in range(depth)] for side in range(2)] for k in range(2)]
    high, base = halves(*tiles[1], 1), halves(*tiles[0], 0)
    groups = [(pay_ref, jnp.concatenate(high, axis=1), -float(SIDE))]
    if merge:
        mine = jnp.where(col == 0, groups[0][1], jnp.concatenate(base, axis=1))
        groups = [(pay_ref, mine, jnp.where(col == 0, -float(SIDE), float(SIDE)))]
    else:
        groups.append((refs[1], jnp.concatenate(base, axis=1), float(SIDE)))
    width = depth * 128
    for ref, tile, shift in groups:
        ref[0:64, 0:width] = tile[0:64]
        x = coordinates(tile[64:80].astype(F32))
        ref[64:80, 0:width] = feature_rows([x[0] + shift, x[1], x[2]])


def tops_kernel(top_ref, out_ref):
    half = out_ref.shape[0]
    for k in range(half):
        out_ref[k] = jnp.concatenate([top_ref[k], top_ref[half + k]], axis=1)


def layers_of(depth, tz):
    return [sz for sz in (tz - 1, tz, tz + 1) if 0 <= sz < depth]


def inner_steps(depth, targets):
    steps = []
    for tz in targets:
        layers = layers_of(depth, tz)
        for sz in layers:
            steps.append((tz, (0, 1), [(sz, 1), (sz, 2)]))
            steps.append((tz, (2, 3), [(sz, 3), (sz, 4)]))
        steps.append((tz, (1,), [(sz, 3) for sz in layers]))
        steps.append((tz, (2,), [(sz, 2) for sz in layers]))
    return steps


def mask_row(mask_ref, at, dz, dy, k, ty):
    row = dz * 16 + dy * 4 + k
    m = mask_ref[at, row : row + 1, 128 * ty : 128 * ty + 128]
    m = jnp.broadcast_to(m, (16, 128)).astype(BF16)
    return jnp.concatenate([m] * 4, axis=0)


AHEAD = 6


def scan(steps, depth, rows_of, charge_of, x_ref, mask_ref, acc_ref, fresh=False):
    steps = [(xp, *step) for xp in range(2) for step in steps]

    def pair():
        ready, seen = [], set()
        for i in range(len(steps) + AHEAD):
            if i < len(steps):
                xp, sides, (tz, tiles, sources) = steps[i]
                lanes = slice(128 * tiles[0], 128 * tiles[-1] + 128)
                at = xp * depth + tz
                rows = jnp.concatenate([rows_of(sides, xp, sz, ye) for sz, ye in sources], axis=0)
                features = x_ref[at, 32:96, lanes] if sides else x_ref[at, 0:32, lanes]
                ready.append(lax.rsqrt(dot(rows, features).astype(BF16)))
            if i >= AHEAD:
                xp, sides, (tz, tiles, sources) = steps[i - AHEAD]
                inv, ready[i - AHEAD] = ready[i - AHEAD], None
                lanes = slice(128 * tiles[0], 128 * tiles[-1] + 128)
                at = xp * depth + tz
                size = 64 if sides else 128
                columns = []
                for j, ty in enumerate(tiles):
                    blocks = []
                    for k, (sz, ye) in enumerate(sources):
                        part = inv[size * k : size * k + size, 128 * j : 128 * j + 128]
                        halves = [part, part] if sides else [part[0:64], part[64:128]]
                        first = 2 if sides else 0
                        blocks += [
                            h * mask_row(mask_ref, at, sz - tz + 1, ye - ty, first + c, ty) for c, h in enumerate(halves)
                        ]
                    columns.append(jnp.concatenate(blocks, axis=0))
                kernel = columns[0] if len(columns) == 1 else jnp.concatenate(columns, axis=1)
                charge = jnp.concatenate([charge_of(sides, xp, sz, ye) for sz, ye in sources], axis=1)
                value = dot(charge, kernel)
                if fresh and len(tiles) == 2 and (xp, tz, tiles) not in seen:
                    seen.add((xp, tz, tiles))
                    acc_ref[at, :, lanes] = value
                else:
                    acc_ref[at, :, lanes] += value

    pair()


def own_kernel(depth, targets, q_ref, feat_ref, nl_ref, sel_ref, sel_x_ref, pick_ref, acc_ref, x_ref, mask_ref, yt_ref):
    columns = q_ref.shape[1]
    leaves = columns // 64
    x = dot(sel_x_ref[...], feat_ref[...])
    active = jnp.where(nl_ref[...] >= 0, 1.0, 0.0).astype(BF16)
    pick = dot(pick_ref[...], active)
    pick = jnp.where(
        lax.broadcasted_iota(jnp.int32, (48, leaves), 1) % 2 == 0, pick[0:48], pick[48:96]
    ).astype(BF16)
    spread = jnp.where(
        lax.broadcasted_iota(jnp.int32, (leaves, columns), 0)
        == lax.broadcasted_iota(jnp.int32, (leaves, columns), 1) // 64,
        1.0,
        0.0,
    ).astype(BF16)
    masks = dot(pick, spread)
    low = lower_half((32, 128))
    rows = dot(feat_ref[...], sel_ref[:, 0:32], TN).astype(BF16)
    for z in range(depth):
        for xp in range(2):
            for y in range(SIDE):
                at = tile_of(z, y, xp) * 128
                lanes = slice(128 * y, 128 * y + 128)
                tile = x[:, at : at + 128]
                x_ref[xp * depth + z, 0:32, lanes] = tile.astype(BF16)
                x_ref[xp * depth + z, 32:64, lanes] = jnp.where(low, 0.0, tile).astype(BF16)
                x_ref[xp * depth + z, 64:96, lanes] = jnp.where(low, tile, 0.0).astype(BF16)
                mask_ref[xp * depth + z, :, lanes] = masks[:, at : at + 128]
                yt_ref[(xp * depth + z) * SIDE + y] = rows[at : at + 128]

    own_steps(depth, targets, q_ref, x_ref, mask_ref, yt_ref, acc_ref)


def own_steps(depth, targets, q_ref, x_ref, mask_ref, yt_ref, acc_ref):
    def rows_of(sides, xp, sz, ye):
        return yt_ref[(xp * depth + sz) * SIDE + ye - 1]

    def charge_of(sides, xp, sz, ye):
        base = tile_of(sz, ye - 1, xp) * 128
        return q_ref[:, base : base + 128]

    steps = [(False, step) for step in inner_steps(depth, targets)]
    scan(steps, depth, rows_of, charge_of, x_ref, mask_ref, acc_ref, fresh=True)


def more_own_kernel(depth, targets, q_ref, x_ref, mask_ref, yt_ref, in_ref, acc_ref):
    own_steps(depth, targets, q_ref, x_ref, mask_ref, yt_ref, acc_ref)


def beside(right, left):
    return jnp.concatenate([right, left], axis=1)


def side_kernel(merge, depth, targets, q_ref, right_ref, *refs):
    if not merge:
        left_ref, *refs = refs
    sel_ref, x_ref, mask_ref, yt_ref, _, acc_ref, c_ref, ys_ref = refs
    low = lower_half((64, 128))
    count = 2 * depth
    rights = tiles_in(right_ref, 0, count)
    lefts = rights if merge else tiles_in(left_ref, 0, count)
    beyond = [tile for pair in unpacked(rights, lefts) for tile in pair]
    turned = transposed([with_ones(h[64:80]) for h in beyond], sel_ref)
    for z in range(depth):
        for y in range(SIDE):
            t = [q_ref[:, a * 128 : a * 128 + 128] for a in (tile_of(z, y, 0), tile_of(z, y, 1))]
            even, odd = z * SIDE + y, (depth + z) * SIDE + y
            h, rows = beyond[even][0:64], turned[even]
            c_ref[even] = jnp.where(low, t[1], h)
            c_ref[odd] = jnp.where(low, h, t[0])
            ys_ref[even] = beside(yt_ref[odd, 0:64], rows[64:128])
            ys_ref[odd] = beside(rows[0:64], yt_ref[even, 64:128])

    side_steps(depth, targets, x_ref, mask_ref, c_ref, ys_ref, acc_ref)


def side_steps(depth, targets, x_ref, mask_ref, c_ref, ys_ref, acc_ref):
    def rows_of(sides, xp, sz, ye):
        return ys_ref[(xp * depth + sz) * SIDE + ye - 1]

    def charge_of(sides, xp, sz, ye):
        return c_ref[(xp * depth + sz) * SIDE + ye - 1]

    steps = [(True, step) for step in inner_steps(depth, targets)]
    scan(steps, depth, rows_of, charge_of, x_ref, mask_ref, acc_ref)


def more_side_kernel(depth, targets, x_ref, mask_ref, c_ref, ys_ref, in_ref, acc_ref):
    side_steps(depth, targets, x_ref, mask_ref, c_ref, ys_ref, acc_ref)


def edge_steps(depth, sides):
    steps = []
    for tz in range(depth):
        for side in range(2):
            sources = [(sz, side * (SIDE + 1)) for sz in layers_of(depth, tz)]
            steps.append((sides, (tz, (side * (SIDE - 1),), sources)))
    return steps


def edge_kernel(depth, even_ref, odd_ref, sel_ref, x_ref, mask_ref, in_ref, acc_ref, c_ref, yt_ref):
    face = row_sides(even_ref, odd_ref)
    places = [(k, z, side) for k in range(2) for z in range(depth) for side in range(2)]
    tiles = [face(side, (z * 2 + k) * 128) for k, z, side in places]
    for i, rows in enumerate(transposed([with_ones(tile[64:80]) for tile in tiles], sel_ref)):
        c_ref[i] = tiles[i][0:64]
        yt_ref[i] = rows

    def rows_of(sides, xp, sz, ye):
        return yt_ref[(xp * depth + sz) * 2 + (ye > 0)]

    def charge_of(sides, xp, sz, ye):
        return c_ref[(xp * depth + sz) * 2 + (ye > 0)]

    scan(edge_steps(depth, False), depth, rows_of, charge_of, x_ref, mask_ref, acc_ref)


def last_kernel(merge, depth, edge_c_ref, edge_y_ref, right_ref, *refs):
    if not merge:
        left_ref, *refs = refs
    sel_ref, x_ref, mask_ref, _, acc_ref, c_ref, ys_ref = refs
    low = lower_half((64, 128))
    rights = tiles_in(right_ref, 0, depth)
    lefts = rights if merge else tiles_in(left_ref, 0, depth)
    beyond = [tile for pair in unpacked(rights, lefts) for tile in pair]
    turned = transposed([with_ones(h[64:80]) for h in beyond], sel_ref)
    for z in range(depth):
        for side in range(2):
            even, odd = z * 2 + side, (depth + z) * 2 + side
            h, rows = beyond[even][0:64], turned[even]
            c_ref[even] = jnp.where(low, edge_c_ref[odd], h)
            c_ref[odd] = jnp.where(low, h, edge_c_ref[even])
            ys_ref[even] = beside(edge_y_ref[odd, 0:64], rows[64:128])
            ys_ref[odd] = beside(rows[0:64], edge_y_ref[even, 64:128])

    def rows_of(sides, xp, sz, ye):
        return ys_ref[(xp * depth + sz) * 2 + (ye > 0)]

    def charge_of(sides, xp, sz, ye):
        return c_ref[(xp * depth + sz) * 2 + (ye > 0)]

    scan(edge_steps(depth, True), depth, rows_of, charge_of, x_ref, mask_ref, acc_ref)


def couple_kernel(merge, group, k1_ref, *refs):
    col = lax.axis_index("col")
    if merge:
        own_ref, got_ref, l1_ref, out_ref, coef_ref = refs
        nodes = l1_ref.shape[0]
        at = got_ref.shape[1] - 256
        got = jnp.concatenate([got_ref[:, at : at + 128], got_ref[:, at + 128 : at + 256]], axis=0)
        for k in range(nodes // 2):
            for side, value in enumerate((own_ref[32 * k : 32 * k + 32, :], got[32 * k : 32 * k + 32])):
                coef_ref[side * nodes + 2 * k] = value[:, 0:64]
                coef_ref[side * nodes + 2 * k + 1] = value[:, 64:128]
        coef_ref[group] = jnp.zeros((32, 64), BF16)
    else:
        coef_ref, l1_ref, out_ref = refs
    nodes, slots = l1_ref.shape
    mask = col * nodes
    zero = jnp.zeros((32, 64), BF16)
    totals = []
    for n in range(nodes):
        parts = []
        for s in range(slots):
            v = l1_ref[n, s]
            at = (v & (group - 1)) ^ mask
            if merge:
                parts.append(coef_ref[jnp.where(v >= 0, at, group)])
            else:
                parts.append(jnp.where(v >= 0, coef_ref[at], zero))
        matrix = jnp.concatenate([k1_ref[n, s] for s in range(slots)], axis=1)
        totals.append(dot(matrix, jnp.concatenate(parts, axis=0)))
    for n in range(nodes):
        out_ref[32 * n : 32 * n + 32, :] = totals[n]


def down_kernel(depth, merge, acc_ref, f1_ref, basis_ref, t1_ref, t2_ref, k2_ref, top_ref, *refs):
    if merge:
        got_ref, *refs = refs
    l2_ref, out_hbm, out_ref, sems, top_scr = refs
    row, col = lax.axis_index("row"), lax.axis_index("col")
    nodes = out_hbm.shape[1] // 512
    per = nodes // 8
    me = row * lax.axis_size("col") + col
    if merge:
        count = top_ref.shape[0]
        bits = count.bit_length() - 1
        place = [sum(((k >> b) & 1) << (bits - 1 - b) for b in range(bits)) for k in range(count)]
        for k in range(count // 2):
            block = got_ref[k]
            top_scr[2 * place[k] + 1] = block[:, 0:64]
            top_scr[2 * place[k + count // 2] + 1] = block[:, 64:128]
        for k in range(count):
            top_scr[2 * place[k]] = top_ref[k]
    else:
        top_scr[...] = top_ref[...]
    copies = []
    for m in range(per):
        parts = []
        for s in range(l2_ref.shape[1]):
            v = l2_ref[m, s]
            at = v ^ me if per == 1 else ((v // per) ^ me) * per + v % per
            parts.append(top_scr[at])
        matrix = jnp.concatenate([k2_ref[m, s] for s in range(l2_ref.shape[1])], axis=1)
        hi2, lo2 = split2(dot(matrix, jnp.concatenate(parts, axis=0)))
        t2 = t2_ref[256 * m : 256 * m + 256, :]
        hi1, lo1 = split2(f1_ref[256 * m : 256 * m + 256, :] + dot(t2, hi2) + dot(t2, lo2))
        leaves = []
        for j in range(8):
            n = 8 * m + j
            t1 = t1_ref[256 * n : 256 * n + 256, :]
            rows = slice(32 * j, 32 * j + 32)
            leaves.append((dot(t1, hi1[rows]) + dot(t1, lo1[rows])).astype(BF16))
        for j in range(8):
            n = 8 * m + j
            far = dot(leaves[j], block_basis(basis_ref[:, 512 * n : 512 * n + 512]), TN)
            z1, y1, x1 = j // 4, j // 2 % 2, j % 2
            for k in range(4):
                z, y = 4 * m + 2 * z1 + k // 2, 2 * y1 + k % 2
                part = acc_ref[x1 * depth + z, :, 128 * y : 128 * y + 128]
                total = part * (NEAR * 64) ** (-0.5) + far[:, 128 * k : 128 * k + 128]
                out_ref[:, 512 * n + 128 * k : 512 * n + 128 * k + 128] = total.astype(BF16)
            lanes = pl.ds(512 * n, 512)
            copies.append(pltpu.make_async_copy(out_ref.at[:, lanes], out_hbm.at[:, lanes], sems.at[n]))
            copies[-1].start()
    for copy in copies:
        copy.wait()


def constants():
    sel = np.zeros((16, 160), np.float32)
    sel_x = np.zeros((32, 16), np.float32)
    rest, eps = np.float32(SOFTENING), []
    for _ in range(3):
        eps.append(np.asarray(rest).astype(jnp.bfloat16).astype(np.float32))
        rest = np.float32(rest - eps[-1])
    for f in range(21):
        source = f if f < 6 else f - 6 if f < 12 else 9 if f < 15 else f - 9 if f < 18 else 9
        for base in (0, 32, 128):
            sel[source, base + f] = 1
        if f < 12:
            sel_x[f, f % 3 + (3 if f >= 6 else 0)] = -2
        elif f < 15:
            sel_x[f, f - 6] = 1
        else:
            sel_x[f, 9] = 1 if f < 18 else eps[f - 18]
    pick = np.zeros((96, NEAR), np.float32)
    for dz in range(3):
        for dy in range(3):
            for k in range(4):
                for half, dx in enumerate(((0, 1, None, -1)[k], (-1, 0, 1, None)[k])):
                    if dx is not None:
                        pick[48 * half + dz * 16 + dy * 4 + k, 9 * dz + 3 * dy + dx + 1] = 1
    return [jnp.asarray(v, BF16) for v in (sel, sel_x, pick)]


def permuted(value, axis, pairs):
    return lax.ppermute(value, axis, pairs)


def doubled(value, axis, start=1):
    size = lax.axis_size(axis)
    step = start
    while step < size:
        other = permuted(value, axis, [(i, i ^ step) for i in range(size)])
        value = jnp.concatenate([value, other], axis=0)
        step *= 2
    return value


def call(kernel, out_shape, ins, smem=0, scratch=(), flops=0, alias=None, hbm_in=0, hbm_out=False):
    single = not isinstance(out_shape, list)
    return pallas(kernel, out_shape, ins, smem, scratch, flops, alias, single, hbm_in, hbm_out)


def pallas(kernel, out_shape, ins, smem, scratch, flops, alias, single, hbm_in, hbm_out):
    return pl.pallas_call(
        kernel,
        out_shape=out_shape,
        in_specs=[HBM] * hbm_in + [VMEM] * (len(ins) - smem - hbm_in) + [SMEM] * smem,
        out_specs=(HBM if hbm_out else VMEM) if single else [VMEM] * len(out_shape),
        scratch_shapes=list(scratch),
        input_output_aliases={alias: 0} if alias is not None else {},
        compiler_params=pltpu.CompilerParams(vmem_limit_bytes=40 * 1024 * 1024),
        cost_estimate=pl.CostEstimate(flops=flops, bytes_accessed=1 << 20, transcendentals=0) if flops else None,
    )(*ins)


def shards(
    charges, points, leaf_basis, transfer_one, transfer_two, couple_one, couple_two, near_list, list_one, list_two
):
    columns = charges.shape[1]
    leaves = near_list.shape[0]
    nodes = leaves // 8
    tops = nodes // 8
    depth = 4 * (leaves // 64)
    rows, cols = lax.axis_size("row"), lax.axis_size("col")
    merge = cols == 2 and tops == 1
    t1 = transfer_one.reshape(leaves * 32, 32)
    t2 = transfer_two.reshape(nodes * 32, 32)
    shape = jax.ShapeDtypeStruct
    width = 2 * depth * 128
    face = shape((80, width), BF16)
    up = [(i, i + 1) for i in range(cols - 1)]
    down = [(j, i) for i, j in up]
    corner_width = depth * 128
    leaf = call(leaf_kernel, shape((nodes, 256, 64), BF16), [charges, leaf_basis], flops=1 << 31)
    ups = call(
        functools.partial(up_kernel, merge),
        [shape((16 * nodes, 128), BF16), shape((1, 32, 64), BF16)]
        if merge
        else [shape(((nodes + tops) * 32, 64), BF16)],
        [leaf, t1, t2],
        flops=1 << 31,
    )
    coef = ups[0]
    outs = call(
        functools.partial(face_kernel, merge, depth),
        [shape((16, columns), BF16), face, face]
        + ([shape((80, width + 256), BF16)] if merge else [face, face]),
        [charges, points] + ([coef] if merge else []),
        flops=1 << 31,
    )
    feat, even, odd, pay = outs[:4]
    odd = permuted(odd, "row", [p for i in range(1, rows - 1, 2) for p in ((i, i + 1), (i + 1, i))])
    even = permuted(even, "row", [(i, i ^ 1) for i in range(rows)])
    if merge:
        left = right = permuted(pay, "col", up + down)
        top = ups[1]
        step = rows // 2
        while step:
            other = permuted(top, "row", [(i, i ^ step) for i in range(rows)])
            top = jnp.concatenate([top, other], axis=0)
            step //= 2
        one = [coef, right]
    else:
        left, right = permuted(pay, "col", up), permuted(outs[4], "col", down)
        coef = doubled(coef.reshape(1, nodes + tops, 32, 64), "col")
        one = [coef[:, :nodes].reshape(cols * nodes, 32, 64)]
        top = doubled(coef[:, nodes:].reshape(1, cols * tops, 32, 64), "row").reshape(-1, 32, 64)
    sel, sel_x, pick = constants()
    acc_shape = shape((2 * depth, 64, 512), F32)
    first, second, third = split_layers(depth)
    acc, x, mask, yt = call(
        functools.partial(own_kernel, depth, first),
        [
            acc_shape,
            shape((2 * depth, 96, 512), BF16),
            shape((2 * depth, 48, 512), F32),
            shape((2 * depth * SIDE, 128, 32), BF16),
        ],
        [charges, feat, near_list.T, sel, sel_x, pick],
        flops=1 << 32,
    )
    for targets in (second, third):
        acc = call(
            functools.partial(more_own_kernel, depth, targets),
            acc_shape,
            [charges, x, mask, yt, acc],
            alias=4,
            flops=1 << 31,
        )
    corner = shape((80, corner_width), BF16)
    packed = call(functools.partial(corner_kernel, merge, depth), [corner] if merge else [corner, corner], [even, odd])
    if merge:
        corner_left = corner_right = permuted(packed[0], "col", up + down)
        got = call(tops_kernel, shape((rows // 2, 32, 128), BF16), [top])
        got = permuted(got, "col", up + down)
    else:
        corner_left = permuted(packed[0], "col", up)
        corner_right = permuted(packed[1], "col", down)
    acc, side_c, side_y = call(
        functools.partial(side_kernel, merge, depth, range(0, depth // 2)),
        [acc_shape, shape((2 * depth * SIDE, 64, 128), BF16), shape((2 * depth * SIDE, 64, 64), BF16)],
        [charges, right] + ([] if merge else [left]) + [sel, x, mask, yt, acc],
        alias=6 if merge else 7,
        flops=1 << 32,
    )
    acc = call(
        functools.partial(more_side_kernel, depth, range(depth // 2, depth)),
        acc_shape,
        [x, mask, side_c, side_y, acc],
        alias=4,
        flops=1 << 31,
    )
    acc, edge_c, edge_y = call(
        functools.partial(edge_kernel, depth),
        [acc_shape, shape((4 * depth, 64, 128), BF16), shape((4 * depth, 128, 32), BF16)],
        [even, odd, sel, x, mask, acc],
        alias=5,
        flops=1 << 31,
    )
    field = call(
        functools.partial(couple_kernel, merge, cols * nodes),
        shape((nodes * 32, 64), F32),
        [couple_one, *one, list_one],
        smem=1,
        scratch=[pltpu.VMEM((2 * nodes + 1, 32, 64), BF16)] if merge else [],
        flops=1 << 30,
    )
    acc = call(
        functools.partial(last_kernel, merge, depth),
        acc_shape,
        [edge_c, edge_y, corner_right] + ([] if merge else [corner_left]) + [sel, x, mask, acc],
        alias=6 if merge else 7,
        scratch=[pltpu.VMEM((4 * depth, 64, 128), BF16), pltpu.VMEM((4 * depth, 64, 64), BF16)],
        flops=1 << 31,
    )
    return call(
        functools.partial(down_kernel, depth, merge),
        shape((64, columns), BF16),
        [acc, field, leaf_basis, t1, t2, couple_two, top] + ([got] if merge else []) + [list_two],
        smem=1,
        scratch=[
            pltpu.VMEM((64, columns), BF16),
            pltpu.SemaphoreType.DMA((nodes,)),
            pltpu.VMEM((rows * cols * tops, 32, 64), BF16),
        ],
        hbm_out=True,
    )


def solution(mesh):
    line, block = P(None, ("row", "col")), P(("row", "col"))
    in_specs = (line, line, line) + (block,) * 7

    return jax.shard_map(shards, mesh=mesh, in_specs=in_specs, out_specs=line, check_vma=False)
```
